128 devices in a mesh: row: 8 (over y_lo, z), col: 2 (over y_hi), tensor: 8 (over x, core).
Axes of the slice: x: 4, y: 4 (y_hi: 2, y_lo: 2; y = y_hi * 2 + y_lo), z: 4, core: 2. Of those that a mesh axis runs over, the one named last changes fastest.
Arguments:
- tokens: bfloat16 [10240, 3072], P(('row', 'col', 'tensor')), may hold values from -6 to 6
- w_query: bfloat16 [3072, 3072], P(None, 'tensor'), may hold values from -0.109375 to 0.109375
- w_key: bfloat16 [3072, 3072], P(None, 'tensor'), may hold values from -0.109375 to 0.109375
- w_value: bfloat16 [3072, 3072], P(None, 'tensor'), may hold values from -0.109375 to 0.109375
- w_out: bfloat16 [3072, 3072], P('tensor'), may hold values from -0.109375 to 0.109375
- w_mod: bfloat16 [512, 18432], P(None, ('row', 'col', 'tensor')), may hold values from -2 to 2
- gain_query: float32 [64], replicated, may hold values from 0.5 to 2.5
- gain_key: float32 [64], replicated, may hold values from 0.5 to 2.5
- timesteps: int32 [2], replicated, may hold values from 0 to 999
- video_lengths: int32 [2], replicated, may hold values from 1 to 6117, 9788 in all
- piece_table: int32 [16], replicated, may hold values from 0 to 15, each once
Outputs:
- update: bfloat16 [10240, 3072], P(('row', 'col', 'tensor'))
The draws below stay inside these ranges and needn't reach their ends.
Inputs may be any that keep to these rules, and one draw needn't show every extreme that they name: `video_lengths`: the two lengths sum to 9788; the larger one is at most 6117, and which sample has it varies. `piece_table`: each tile index 0 .. 15 appears once.
All inputs are finite; a program needn't handle non-finite values.
Results may differ from the reference program's by a relative error of at most 0.02.
Values may be sent and summed in bfloat16 or wider, within the bound.
No kernel may reach another device: no remote copies, remote signals or barrier semaphores. Data moves between devices by JAX's collectives and lax.ppermute only.
A program may use at most 192 MiB of HBM per device.

```python
import math
import jax
import jax.numpy as jnp
import numpy as np
from jax import lax

D = 3072
HEADS = 48
HD = 64
TE = 512
TEXT = 226
HP = 30
WP = 45
CAP = 640
TILES = 16
SLOTS = 10240
VID = 9788
LONGEST = 6117


def steps_of(rng, extent, split, low, high):
    factor_of = 1.0
    for position, shards_of in split:
        steps = jax.random.uniform(jax.random.fold_in(jax.random.fold_in(rng, 6), position), (shards_of,), jnp.float32, low / len(split), high / len(split))
        factor_of = factor_of * jnp.repeat(jnp.exp(steps), extent[position] // shards_of).reshape((-1,) + (1,) * (len(extent) - 1 - position))
    return factor_of


def profile(count, total, limit, lean):
    portions = [(1 << 20) // math.isqrt(grade ** lean) + 1 for grade in range(2, count + 1)]
    spare, given = total - limit - (count - 1), [1] * (count - 1)
    while spare > 0:
        movable = [i for i in range(count - 1) if given[i] < limit]
        pool, budget = sum([portions[i] for i in movable]), spare
        for i in movable:
            extra = min(limit - given[i], max(1, budget * portions[i] // pool), spare)
            given[i] = given[i] + extra
            spare = spare - extra
    return np.array([limit] + given)


def ragged_sizes(rng, amount, total, bound, skew):
    if amount == 2:
        one = jax.random.randint(rng, (), max(1, total - bound), min(bound, total - 1) + 1)
        return jnp.stack([one, total - one])
    lengths = jnp.asarray(profile(amount, total, bound, skew), jnp.int32)
    couples = (amount - 1) // 2
    donor, receiver = lengths[1:1 + 2 * couples:2], lengths[2:2 + 2 * couples:2]
    slack = jnp.minimum(donor - 1, bound - receiver)
    moved = jax.random.randint(jax.random.fold_in(rng, 1), (couples,), 0, 1 << 20) % (slack + 1)
    lengths = lengths.at[1:1 + 2 * couples:2].set(donor - moved).at[2:2 + 2 * couples:2].set(receiver + moved)
    return lengths[jax.random.permutation(jax.random.fold_in(rng, 2), amount)]


def centred(key, dims, spread, bound, cuts=(), kind=jnp.bfloat16):
    result = spread * jax.random.normal(key, dims, jnp.float32)
    if cuts:
        result = result * steps_of(key, dims, cuts, -0.22, 0.18)
    return jnp.clip(result, -bound, bound).astype(kind)


def setup_inputs(seed: int = 0) -> dict:
    streams_of = jax.random.split(jax.random.key(seed), 12)
    tokens = centred(streams_of[0], (SLOTS, D), 1.0, 6.0, ((0, 128),))
    w_query = centred(streams_of[1], (D, D), D ** -0.5, 0.109375, ((1, 8),))
    w_key = centred(streams_of[2], (D, D), D ** -0.5, 0.109375, ((1, 8),))
    w_value = centred(streams_of[3], (D, D), D ** -0.5, 0.109375, ((1, 8),))
    w_out = centred(streams_of[4], (D, D), D ** -0.5, 0.109375, ((0, 8),))
    w_mod = centred(streams_of[5], (TE, 6 * D), 0.15, 2.0, ((1, 128),))
    gain_query = jnp.clip(jnp.exp(jax.random.uniform(streams_of[6], (HD,), jnp.float32, math.log(0.5), math.log(2.5))), 0.5, 2.5)
    gain_key = jnp.clip(jnp.exp(jax.random.uniform(streams_of[7], (HD,), jnp.float32, math.log(0.5), math.log(2.5))), 0.5, 2.5)
    timesteps = jax.random.randint(streams_of[8], (2,), 0, 1000).astype(jnp.int32)
    video_lengths = ragged_sizes(streams_of[9], 2, VID, LONGEST, 0).astype(jnp.int32)
    piece_table = jax.random.permutation(streams_of[10], TILES).astype(jnp.int32)
    return {"tokens": tokens, "w_query": w_query, "w_key": w_key, "w_value": w_value, "w_out": w_out, "w_mod": w_mod, "gain_query": gain_query, "gain_key": gain_key, "timesteps": timesteps, "video_lengths": video_lengths, "piece_table": piece_table}


def slot_info(slot_ids, piece_table, video_lengths):
    tile_idx = slot_ids // CAP
    token_id = piece_table[tile_idx] * CAP + slot_ids % CAP
    boundary = TEXT + video_lengths[0]
    item_of = (token_id >= boundary).astype(jnp.int32)
    inner_idx = token_id - item_of * boundary
    is_text = inner_idx < TEXT
    video_idx = jnp.maximum(inner_idx - TEXT, 0)
    frame_idx = video_idx // (HP * WP)
    height_idx = video_idx // WP % HP
    width_idx = video_idx % WP
    return (item_of, is_text, frame_idx, height_idx, width_idx)

def time_features(timesteps):
    half_dim = TE // 2
    freqs = jnp.exp(-math.log(10000.0) * jnp.arange(half_dim, dtype=jnp.float32) / half_dim)
    angles = timesteps.astype(jnp.float32)[:, None] * freqs[None, :]
    return jnp.concatenate([jnp.cos(angles), jnp.sin(angles)], axis=1)

def rope_angles(frame_idx, height_idx, width_idx):
    time_dims = HD // 4
    space_dims = 3 * HD // 8
    freq_time = 10000.0 ** (-jnp.arange(0, time_dims, 2, dtype=jnp.float32) / time_dims)
    freq_space = 10000.0 ** (-jnp.arange(0, space_dims, 2, dtype=jnp.float32) / space_dims)
    return jnp.concatenate([frame_idx.astype(jnp.float32)[:, None] * freq_time[None, :], height_idx.astype(jnp.float32)[:, None] * freq_space[None, :], width_idx.astype(jnp.float32)[:, None] * freq_space[None, :]], axis=1)

def head_prepare(projection, gain, angles, is_text):
    row_count = projection.shape[0]
    heads_here = projection.shape[1] // HD
    per_head = projection.reshape(row_count, heads_here, HD)
    center = per_head - lax.optimization_barrier(jnp.mean(per_head, axis=2, keepdims=True))
    variance = lax.optimization_barrier(jnp.mean(center * center, axis=2, keepdims=True))
    normed = center * lax.rsqrt(variance + 1e-06) * gain
    cosine = jnp.where(is_text[:, None], 1.0, jnp.cos(angles))[:, None, :]
    sine = jnp.where(is_text[:, None], 0.0, jnp.sin(angles))[:, None, :]
    paired = normed.reshape(row_count, heads_here, HD // 2, 2)
    even_part = paired[..., 0]
    odd_part = paired[..., 1]
    rotated = jnp.stack([even_part * cosine - odd_part * sine, even_part * sine + odd_part * cosine], axis=-1)
    return rotated.reshape(row_count, heads_here * HD).astype(jnp.bfloat16)

def select_modulation(modulation, item_of, is_text, model_width):
    chosen = []
    for part_idx in range(3):
        video_cols = modulation[:, part_idx * model_width:(part_idx + 1) * model_width]
        text_cols = modulation[:, (part_idx + 3) * model_width:(part_idx + 4) * model_width]
        video_pick = jnp.where(item_of[:, None] == 1, video_cols[1][None, :], video_cols[0][None, :])
        text_pick = jnp.where(item_of[:, None] == 1, text_cols[1][None, :], text_cols[0][None, :])
        chosen.append(jnp.where(is_text[:, None], text_pick, video_pick))
    return (chosen[0], chosen[1], chosen[2])

def modulate(tokens, shift, scale):
    values = tokens.astype(jnp.float32)
    center = values - lax.optimization_barrier(jnp.mean(values, axis=1, keepdims=True))
    variance = lax.optimization_barrier(jnp.mean(center * center, axis=1, keepdims=True))
    normed = center * lax.rsqrt(variance + 1e-05)
    return (normed * (1.0 + scale) + shift).astype(jnp.bfloat16)

def reference(tokens, w_query, w_key, w_value, w_out, w_mod, gain_query, gain_key, timesteps, video_lengths, piece_table):
    slot_ids = jnp.arange(SLOTS, dtype=jnp.int32)
    item_of, is_text, frame_idx, height_idx, width_idx = slot_info(slot_ids, piece_table, video_lengths)
    act = jax.nn.silu(time_features(timesteps)).astype(jnp.bfloat16)
    modulation = jnp.dot(act, w_mod, preferred_element_type=jnp.float32)
    shift, scale, gate = select_modulation(modulation, item_of, is_text, D)
    modded = modulate(tokens, shift, scale)
    angles = rope_angles(frame_idx, height_idx, width_idx)
    query = head_prepare(jnp.dot(modded, w_query, preferred_element_type=jnp.float32), gain_query, angles, is_text)
    key_rows = head_prepare(jnp.dot(modded, w_key, preferred_element_type=jnp.float32), gain_key, angles, is_text)
    value_rows = jnp.dot(modded, w_value, preferred_element_type=jnp.float32).astype(jnp.bfloat16)
    key_heads = key_rows.reshape(SLOTS, HEADS, HD).transpose(1, 0, 2)
    value_heads = value_rows.reshape(SLOTS, HEADS, HD).transpose(1, 0, 2)
    query_blocks = query.reshape(TILES, CAP, D)
    item_blocks = item_of.reshape(TILES, CAP)

    def one_block(block):
        query_block, query_item = block
        query_heads = query_block.reshape(CAP, HEADS, HD).transpose(1, 0, 2)
        same_item = (query_item[:, None] == item_of[None, :]).astype(jnp.float32)

        def one_head(head):
            query_head, key_head, value_head = head
            scores = jnp.dot(query_head, key_head.T, preferred_element_type=jnp.float32) / math.sqrt(HD)
            weights = (jnp.exp(scores) * same_item).astype(jnp.bfloat16)
            numerator = jnp.dot(weights, value_head, preferred_element_type=jnp.float32)
            denominator = lax.optimization_barrier(jnp.sum(weights.astype(jnp.float32), axis=1))
            return numerator / denominator[:, None]
        outputs = lax.map(one_head, (query_heads, key_heads, value_heads))
        return outputs.transpose(1, 0, 2).reshape(CAP, D).astype(jnp.bfloat16)
    attended = lax.map(one_block, (query_blocks, item_blocks)).reshape(SLOTS, D)
    projected = jnp.dot(attended, w_out, preferred_element_type=jnp.float32)
    return (gate * projected).astype(jnp.bfloat16)
```

```python
import functools
import math

import jax
import jax.numpy as jnp
from jax import lax
from jax.experimental import pallas as pl
from jax.experimental.pallas import tpu as pltpu
from jax.sharding import Mesh, PartitionSpec as P

HD = 64
TE = 512
TEXT = 226
HP = 30
WP = 45
CAP = 640
D = 3072
BLK = 128
OWN = 80
BIG = 16384.0
F32 = jnp.float32
BF16 = jnp.bfloat16

AXES = ("ylo", "z", "yhi", "x", "core")
Y_AXES = ("ylo", "yhi")
Y_INDEX = (0, 2, 1, 3)
VMEM_LIMIT = 60 * 1024 * 1024
SHIFTS = (1, -1, 2)


def shift_x(value, step):
    return lax.ppermute(value, "x", [(i, (i + step) % 4) for i in range(4)])


def shift_z(value, step):
    return lax.ppermute(value, "z", [(i, (i + step) % 4) for i in range(4)])


def shift_y(value, step):
    return lax.ppermute(value, Y_AXES, [(Y_INDEX[i], Y_INDEX[(i + step) % 4]) for i in range(4)])


def swap_core(value):
    return lax.ppermute(value, "core", [(0, 1), (1, 0)])


def time_features(timesteps):
    half_dim = TE // 2
    freqs = jnp.exp(-math.log(10000.0) * jnp.arange(half_dim, dtype=F32) / half_dim)
    angles = timesteps.astype(F32)[:, None] * freqs[None, :]
    return jnp.concatenate([jnp.cos(angles), jnp.sin(angles)], axis=1)


def rope_tables(piece, boundary):
    token = piece * CAP + lax.broadcasted_iota(jnp.int32, (CAP, 2 * HD), 0)
    lane = lax.broadcasted_iota(jnp.int32, (CAP, 2 * HD), 1)
    inner = token - jnp.where(token >= boundary, boundary, 0)
    is_text = inner < TEXT
    video = jnp.maximum(inner - TEXT, 0)
    frame = video // (HP * WP)
    height = video // WP % HP
    width = video % WP
    pair = lane % HD // 2
    time_pairs = HD // 8
    space_pairs = 3 * HD // 16
    freq_time = 10000.0 ** (-jnp.arange(0, HD // 4, 2, dtype=F32) / (HD // 4))
    freq_space = 10000.0 ** (-jnp.arange(0, 3 * HD // 8, 2, dtype=F32) / (3 * HD // 8))
    freq = jnp.concatenate([freq_time, freq_space, freq_space])
    freq = jnp.tile(jnp.repeat(freq, 2), 2)[None, :]
    place = jnp.where(
        pair < time_pairs, frame, jnp.where(pair < time_pairs + space_pairs, height, width)
    )
    angle = place.astype(F32) * freq
    cosine = jnp.where(is_text, 1.0, jnp.cos(angle))
    sine = jnp.where(is_text, 0.0, jnp.sin(angle))
    return cosine, jnp.where(lane % 2 == 0, -sine, sine)


def project_kernel(
    info, c0, c1, c2, c3, c4, c5, c6, c7, mods, wq, wk, wv, cos, sin, gq, gk,
    qa, kva, qb, kvb, rows_in, middle,
):
    chunks = (c0, c1, c2, c3, c4, c5, c6, c7)
    for i, chunk in enumerate(chunks):
        rows_in[pl.ds(pl.multiple_of(info[i], 16), OWN), :] = chunk[...]
    piece = info[8]
    boundary = info[9]
    line = lax.broadcasted_iota(jnp.int32, (2 * HD, 2 * HD), 0)
    lane = lax.broadcasted_iota(jnp.int32, (2 * HD, 2 * HD), 1)
    average = jnp.where(line // HD == lane // HD, 1.0 / HD, 0.0)
    even = lane % 2 == 0

    def head_prepare(value, gain, block):
        mean = jnp.dot(value, average, precision=lax.Precision.HIGHEST)
        center = value - mean
        variance = jnp.dot(center * center, average, precision=lax.Precision.HIGHEST)
        normed = center * lax.rsqrt(variance + 1e-06) * gain[...]
        other = jnp.where(
            even, pltpu.roll(normed, 2 * HD - 1, 1), pltpu.roll(normed, 1, 1)
        )
        place = slice(block * BLK, (block + 1) * BLK)
        return normed * cos[place, :] + other * sin[place, :]

    for block in range(CAP // BLK):
        place = slice(block * BLK, (block + 1) * BLK)
        values = rows_in[place, :].astype(F32)
        center = values - jnp.mean(values, axis=1, keepdims=True)
        variance = jnp.mean(center * center, axis=1, keepdims=True)
        normed = center * lax.rsqrt(variance + 1e-05)
        token = piece * CAP + block * BLK + lax.broadcasted_iota(jnp.int32, (BLK, 1), 0)
        second = token >= boundary
        text = token - jnp.where(second, boundary, 0) < TEXT

        def pick(part):
            video_cols = slice(part * D, (part + 1) * D)
            text_cols = slice((part + 3) * D, (part + 4) * D)
            video_pick = jnp.where(second, mods[1:2, video_cols], mods[0:1, video_cols])
            text_pick = jnp.where(second, mods[1:2, text_cols], mods[0:1, text_cols])
            return jnp.where(text, text_pick, video_pick)

        modded = (normed * (1.0 + pick(1)) + pick(0)).astype(BF16)
        query = jnp.dot(modded, wq[...], preferred_element_type=F32)
        key = jnp.dot(modded, wk[...], preferred_element_type=F32)
        value = jnp.dot(modded, wv[...], preferred_element_type=F32)
        base = block * 192
        for group in range(3):
            cols = slice(group * 128, (group + 1) * 128)
            q_turn = head_prepare(query[:, cols], gq, block).T.astype(BF16)
            v_turn = value[:, cols].T.astype(BF16)
            k_rows = head_prepare(key[:, cols], gk, block)
            if group == 0:
                qa[base : base + 128, :] = q_turn
                kva[960 + base : 960 + base + 128, :] = v_turn
                kva[place, :] = k_rows.astype(BF16)
            elif group == 1:
                qa[base + 128 : base + 192, :] = q_turn[:64]
                qb[base + 128 : base + 192, :] = q_turn[64:]
                kva[960 + base + 128 : 960 + base + 192, :] = v_turn[:64]
                kvb[960 + base + 128 : 960 + base + 192, :] = v_turn[64:]
                middle[place, :] = k_rows
            else:
                qb[base : base + 128, :] = q_turn
                kvb[960 + base : 960 + base + 128, :] = v_turn
                kvb[place, :] = k_rows.astype(BF16)
    left = lax.broadcasted_iota(jnp.int32, (CAP // 2, 2 * HD), 1) < HD
    upper = middle[: CAP // 2, :]
    lower = middle[CAP // 2 :, :]
    kva[CAP:960, :] = jnp.where(left, upper, pltpu.roll(lower, HD, 1)).astype(BF16)
    kvb[CAP:960, :] = jnp.where(left, pltpu.roll(upper, HD, 1), lower).astype(BF16)


def project(info, chunks, mods, wq, wk, wv, cos, sin, gq, gk):
    vmem = pl.BlockSpec(memory_space=pltpu.VMEM)
    return pl.pallas_call(
        project_kernel,
        out_shape=[
            jax.ShapeDtypeStruct((960, 128), BF16),
            jax.ShapeDtypeStruct((1920, 128), BF16),
            jax.ShapeDtypeStruct((960, 128), BF16),
            jax.ShapeDtypeStruct((1920, 128), BF16),
        ],
        in_specs=[pl.BlockSpec(memory_space=pltpu.SMEM)] + [vmem] * 16,
        out_specs=[vmem] * 4,
        scratch_shapes=[pltpu.VMEM((CAP, D), BF16), pltpu.VMEM((CAP, 128), F32)],
        compiler_params=pltpu.CompilerParams(vmem_limit_bytes=VMEM_LIMIT),
        name="project",
    )(info, *chunks, mods, wq, wk, wv, cos, sin, gq, gk)


def attend_kernel(
    limits, q0, q1, q2, q3, k0, k1, k2, k3, own, out1, out2, out3, qs, ks, vs, acc, todo
):
    queries = (q0, q1, q2, q3)
    keys = (k0, k1, k2, k3)
    outs = (None, out1, out2, out3)
    scale = math.log2(math.e) / math.sqrt(HD)
    line = lax.broadcasted_iota(jnp.int32, (CAP, 128), 0)
    lane = lax.broadcasted_iota(jnp.int32, (CAP, 128), 1)
    sub = lane % HD
    q_line = lax.broadcasted_iota(jnp.int32, (HD, CAP), 0)
    q_lane = lax.broadcasted_iota(jnp.int32, (HD, CAP), 1)
    ones = jnp.where(lax.broadcasted_iota(jnp.int32, (16, CAP), 0) == 0, 1.0, 0.0).astype(BF16)
    left = lane < HD
    for tile in range(4):
        second = line >= limits[4 + tile]
        mark = jnp.where(
            sub == 0,
            jnp.where(second, BIG, 0.0),
            jnp.where(sub == 1, jnp.where(second, 0.0, BIG), 0.0),
        ).astype(BF16)
        pair = keys[tile][:CAP, :]
        ks[0, tile] = jnp.where(left, pair, mark)
        ks[1, tile] = jnp.where(left, mark, pair)
        last = keys[tile][CAP:960, :]
        half = CAP // 2
        ks[2, tile, :half, :] = jnp.where(left[:half], last, mark[:half])
        turned = jnp.concatenate([last[:, HD:], last[:, :HD]], axis=1)
        ks[2, tile, half:, :] = jnp.where(left[:half], turned, mark[half:])
        q_second = q_lane >= limits[tile]
        q_mark = jnp.where(
            q_line == 0,
            jnp.where(q_second, 0.0, -1.0),
            jnp.where(q_line == 1, jnp.where(q_second, -1.0, 0.0), 0.0),
        ).astype(BF16)
        for head in range(3):
            at = HD if head == 1 else 0
            qs[head, tile, HD - at : 2 * HD - at, :] = q_mark
            vs[head, tile, HD:, :] = ones
            for block in range(5):
                rows = slice(192 * block + HD * head, 192 * block + HD * head + HD)
                v_rows = slice(960 + rows.start, 960 + rows.stop)
                cols = slice(128 * block, 128 * block + 128)
                qs[head, tile, at : at + HD, cols] = queries[tile][rows, :]
                vs[head, tile, :HD, cols] = keys[tile][v_rows, :]

    for tile in range(4):
        q_first = limits[tile] > 0
        q_rest = limits[tile] < CAP
        count = jnp.int32(0)
        for place in range(4):
            k_first = limits[4 + place] > 0
            k_rest = limits[4 + place] < CAP
            todo[tile * 4 + count] = place
            shared = (q_first & k_first) | (q_rest & k_rest)
            count = count + jnp.where(shared, 1, 0)
        todo[16 + tile] = count

    def part(tile, head, place):
        scores = jnp.dot(ks[head, place], qs[head, tile], preferred_element_type=F32)
        weights = jnp.exp2(scores * scale).astype(BF16)
        return jnp.dot(vs[head, place], weights, preferred_element_type=F32)

    def q_tile(index, carry):
        tile = 3 - index
        count = todo[16 + tile]
        acc[...] = jnp.zeros_like(acc)

        def two(step, inner):
            here = todo[tile * 4 + 2 * step]
            there = todo[tile * 4 + 2 * step + 1]
            for head in range(3):
                acc[head] += part(tile, head, here) + part(tile, head, there)
            return inner

        lax.fori_loop(0, count // 2, two, 0)

        @pl.when(count % 2 == 1)
        def _():
            here = todo[tile * 4 + count - 1]
            for head in range(3):
                acc[head] += part(tile, head, here)

        for place in range(1, 4):

            @pl.when(tile == place)
            def _():
                ref = outs[place]
                sums = jnp.concatenate([acc[head, HD : HD + 1, :] for head in range(3)], axis=0)
                high = sums.astype(BF16)
                low = (sums - high.astype(F32)).astype(BF16)
                for head in range(3):
                    ref[HD * head : HD * head + HD, :] = acc[head, :HD, :].astype(BF16)
                ref[192:195, :] = high
                ref[195:198, :] = low
                ref[198:208, :] = jnp.zeros((10, CAP), BF16)

        @pl.when(tile == 0)
        def _():
            own[...] = acc[...]

        return carry

    lax.fori_loop(0, 4, q_tile, 0)


def attend(limits, queries, keys, name):
    vmem = pl.BlockSpec(memory_space=pltpu.VMEM)
    return pl.pallas_call(
        attend_kernel,
        out_shape=[jax.ShapeDtypeStruct((3, 80, CAP), F32)]
        + [jax.ShapeDtypeStruct((208, CAP), BF16)] * 3,
        in_specs=[pl.BlockSpec(memory_space=pltpu.SMEM)] + [vmem] * 8,
        out_specs=[vmem] * 4,
        scratch_shapes=[
            pltpu.VMEM((3, 4, 128, CAP), BF16),
            pltpu.VMEM((3, 4, CAP, 128), BF16),
            pltpu.VMEM((3, 4, 80, CAP), BF16),
            pltpu.VMEM((3, 80, CAP), F32),
            pltpu.SMEM((24,), jnp.int32),
        ],
        compiler_params=pltpu.CompilerParams(vmem_limit_bytes=VMEM_LIMIT),
        name=name,
    )(limits, *queries, *keys)


def output_kernel(
    order, own_a, a1, a2, a3, own_b, b1, b2, b3, w_out, theirs, mine, turned, rows, picked
):
    for own, others, heads in (
        (own_a, (a1, a2, a3), (0, 1, 2)),
        (own_b, (b1, b2, b3), (4, 5, 3)),
    ):
        for place, head in enumerate(heads):
            total = own[place, :HD, :]
            share = own[place, HD : HD + 1, :]
            for ref in others:
                total = total + ref[HD * place : HD * place + HD, :].astype(F32)
                tail = ref[192:208, :].astype(F32)
                share = share + tail[place : place + 1, :] + tail[3 + place : 4 + place, :]
            turned[HD * head : HD * head + HD, :] = total / share
    for block in range(5):
        place = slice(block * 128, block * 128 + 128)
        for group in range(3):
            cols = slice(group * 128, group * 128 + 128)
            rows[place, cols] = turned[cols, place].T.astype(BF16)
    for i in range(8):
        start = pl.multiple_of(order[i], 16)
        picked[i * OWN : (i + 1) * OWN, :] = rows[pl.ds(start, OWN), :]
    theirs[...] = jnp.dot(picked[: 4 * OWN, :], w_out[...], preferred_element_type=F32).astype(BF16)
    mine[...] = jnp.dot(picked[4 * OWN :, :], w_out[...], preferred_element_type=F32).astype(BF16)


def output(order, own_a, others_a, own_b, others_b, w_out):
    vmem = pl.BlockSpec(memory_space=pltpu.VMEM)
    return pl.pallas_call(
        output_kernel,
        out_shape=[jax.ShapeDtypeStruct((4 * OWN, D), BF16)] * 2,
        in_specs=[pl.BlockSpec(memory_space=pltpu.SMEM)] + [vmem] * 9,
        out_specs=[vmem] * 2,
        scratch_shapes=[
            pltpu.VMEM((384, CAP), F32),
            pltpu.VMEM((CAP, 384), BF16),
            pltpu.VMEM((CAP, 384), BF16),
        ],
        compiler_params=pltpu.CompilerParams(vmem_limit_bytes=VMEM_LIMIT),
        name="output",
    )(order, own_a, *others_a, own_b, *others_b, w_out)


def select_gate(modulation, second, text):
    video_cols = modulation[:, 2 * D : 3 * D]
    text_cols = modulation[:, 5 * D : 6 * D]
    video_pick = jnp.where(second, video_cols[1][None, :], video_cols[0][None, :])
    text_pick = jnp.where(second, text_cols[1][None, :], text_cols[0][None, :])
    return jnp.where(text, text_pick, video_pick)


def local(
    tokens, w_query, w_key, w_value, w_out, w_mod, gain_query, gain_key, timesteps,
    video_lengths, piece_table,
):
    x, core = lax.axis_index("x"), lax.axis_index("core")
    z = lax.axis_index("z")
    y = lax.axis_index("yhi") * 2 + lax.axis_index("ylo")
    boundary = TEXT + video_lengths[0]

    across = [tokens] + [shift_x(tokens, step) for step in SHIFTS]
    chunks = across + [swap_core(chunk) for chunk in across]

    act = jax.nn.silu(time_features(timesteps)).astype(BF16)
    part_mod = jnp.dot(act, w_mod, preferred_element_type=F32)
    width = part_mod.shape[1]
    packed = jnp.pad(part_mod.reshape(2 * width), (0, 384 - 2 * width)).reshape(3, 128)
    spread = lax.all_to_all(
        jnp.broadcast_to(packed[None], (128, 3, 128)), AXES, 0, 0, tiled=True
    ).reshape(128, 384)
    modulation = jnp.stack(
        [spread[:, :width].reshape(128 * width), spread[:, width : 2 * width].reshape(128 * width)]
    )

    back = jnp.array([0, 1, -1, 2], jnp.int32)
    z_ring = (z - back) % 4
    y_ring = (y - back) % 4
    z_tiles = ((y % 2) * 4 + z_ring) * 2 + y // 2
    y_tiles = ((y_ring % 2) * 4 + z) * 2 + y_ring // 2
    tiles = jnp.concatenate([z_tiles, y_tiles])
    pieces = jnp.sum(
        jnp.where(
            tiles[:, None] == jnp.arange(16, dtype=jnp.int32)[None, :], piece_table[None, :], 0
        ),
        axis=1,
    )
    limits_a = jnp.clip(boundary - pieces * CAP, 0, CAP)
    limits_b = jnp.concatenate([limits_a[4:], limits_a[:4]])
    piece = pieces[0]
    x_ring = (x - back) % 4
    starts = jnp.concatenate([(x_ring * 2 + core) * OWN, (x_ring * 2 + 1 - core) * OWN])
    info = jnp.concatenate([starts, jnp.stack([piece, boundary])])

    cos, sin = rope_tables(piece, boundary)
    gq = jnp.tile(gain_query, 2)[None, :]
    gk = jnp.tile(gain_key, 2)[None, :]
    qa, kva, qb, kvb = project(
        info, chunks, modulation, w_query, w_key, w_value, cos, sin, gq, gk
    )

    qa_all = [qa] + [shift_z(qa, step) for step in SHIFTS]
    kva_all = [kva] + [shift_y(kva, step) for step in SHIFTS]
    qb_all = [qb] + [shift_y(qb, step) for step in SHIFTS]
    kvb_all = [kvb] + [shift_z(kvb, step) for step in SHIFTS]
    own_a, *parts_a = attend(limits_a, qa_all, kva_all, "attend_a")
    sent_a = [shift_z(part, -step) for part, step in zip(parts_a, SHIFTS)]
    own_b, *parts_b = attend(limits_b, qb_all, kvb_all, "attend_b")
    sent_b = [shift_y(part, -step) for part, step in zip(parts_b, SHIFTS)]

    ahead = (x + back) % 4
    order = jnp.concatenate([(ahead * 2 + 1 - core) * OWN, (ahead * 2 + core) * OWN])
    theirs, mine = output(order, own_a, sent_a, own_b, sent_b, w_out)
    received = swap_core(theirs)
    total = mine.astype(F32) + received.astype(F32)
    projection = total[:OWN]
    for i, step in enumerate(SHIFTS):
        piece_sum = total[(i + 1) * OWN : (i + 2) * OWN].astype(BF16)
        projection = projection + shift_x(piece_sum, step).astype(F32)

    own_token = piece * CAP + starts[0] + jnp.arange(OWN, dtype=jnp.int32)[:, None]
    second = own_token >= boundary
    text = own_token - jnp.where(second, boundary, 0) < TEXT
    gate = select_gate(modulation, second, text)
    return (gate * projection).astype(BF16)


def solution(mesh):
    fine = Mesh(mesh.devices.reshape(2, 4, 2, 4, 2), AXES)
    tensor = ("x", "core")
    placed = (
        P(AXES, None),
        P(None, tensor),
        P(None, tensor),
        P(None, tensor),
        P(tensor, None),
        P(None, AXES),
        P(),
        P(),
        P(),
        P(),
        P(),
    )
    return jax.shard_map(
        local, mesh=fine, in_specs=placed, out_specs=P(AXES, None), check_vma=False
    )
```

```python
import functools
import math

import jax
import jax.numpy as jnp
from jax import lax
from jax.experimental import pallas as pl
from jax.experimental.pallas import tpu as pltpu
from jax.sharding import Mesh, PartitionSpec as P

HD = 64
TE = 512
TEXT = 226
HP = 30
WP = 45
CAP = 640
D = 3072
BLK = 128
OWN = 80
BIG = 16384.0
F32 = jnp.float32
BF16 = jnp.bfloat16

AXES = ("ylo", "z", "yhi", "x", "core")
Y_AXES = ("ylo", "yhi")
Y_INDEX = (0, 2, 1, 3)
VMEM_LIMIT = 60 * 1024 * 1024
SHIFTS = (1, -1, 2)


def shift_x(value, step):
    return lax.ppermute(value, "x", [(i, (i + step) % 4) for i in range(4)])


def shift_z(value, step):
    return lax.ppermute(value, "z", [(i, (i + step) % 4) for i in range(4)])


def shift_y(value, step):
    return lax.ppermute(value, Y_AXES, [(Y_INDEX[i], Y_INDEX[(i + step) % 4]) for i in range(4)])


def swap_core(value):
    return lax.ppermute(value, "core", [(0, 1), (1, 0)])


def time_features(timesteps):
    half_dim = TE // 2
    freqs = jnp.exp(-math.log(10000.0) * jnp.arange(half_dim, dtype=F32) / half_dim)
    angles = timesteps.astype(F32)[:, None] * freqs[None, :]
    return jnp.concatenate([jnp.cos(angles), jnp.sin(angles)], axis=1)


def rope_tables(piece, boundary):
    token = piece * CAP + lax.broadcasted_iota(jnp.int32, (CAP, 2 * HD), 0)
    lane = lax.broadcasted_iota(jnp.int32, (CAP, 2 * HD), 1)
    inner = token - jnp.where(token >= boundary, boundary, 0)
    is_text = inner < TEXT
    video = jnp.maximum(inner - TEXT, 0)
    frame = video // (HP * WP)
    height = video // WP % HP
    width = video % WP
    pair = lane % HD // 2
    time_pairs = HD // 8
    space_pairs = 3 * HD // 16
    freq_time = 10000.0 ** (-jnp.arange(0, HD // 4, 2, dtype=F32) / (HD // 4))
    freq_space = 10000.0 ** (-jnp.arange(0, 3 * HD // 8, 2, dtype=F32) / (3 * HD // 8))
    freq = jnp.concatenate([freq_time, freq_space, freq_space])
    freq = jnp.tile(jnp.repeat(freq, 2), 2)[None, :]
    place = jnp.where(
        pair < time_pairs, frame, jnp.where(pair < time_pairs + space_pairs, height, width)
    )
    angle = place.astype(F32) * freq
    cosine = jnp.where(is_text, 1.0, jnp.cos(angle))
    sine = jnp.where(is_text, 0.0, jnp.sin(angle))
    return cosine, jnp.where(lane % 2 == 0, -sine, sine)


def project_kernel(
    info, c0, c1, c2, c3, c4, c5, c6, c7, mods, wq, wk, wv, cos, sin, gq, gk,
    along_z, along_y, rows_in, middle,
):
    qa, kvb = along_z.at[:960], along_z.at[960:]
    qb, kva = along_y.at[:960], along_y.at[960:]
    chunks = (c0, c1, c2, c3, c4, c5, c6, c7)
    for i, chunk in enumerate(chunks):
        rows_in[pl.ds(pl.multiple_of(info[i], 16), OWN), :] = chunk[...]
    piece = info[8]
    boundary = info[9]
    line = lax.broadcasted_iota(jnp.int32, (2 * HD, 2 * HD), 0)
    lane = lax.broadcasted_iota(jnp.int32, (2 * HD, 2 * HD), 1)
    average = jnp.where(line // HD == lane // HD, 1.0 / HD, 0.0)
    even = lane % 2 == 0

    def head_prepare(value, gain, block):
        mean = jnp.dot(value, average, precision=lax.Precision.HIGHEST)
        center = value - mean
        variance = jnp.dot(center * center, average, precision=lax.Precision.HIGHEST)
        normed = center * lax.rsqrt(variance + 1e-06) * gain[...]
        other = jnp.where(
            even, pltpu.roll(normed, 2 * HD - 1, 1), pltpu.roll(normed, 1, 1)
        )
        place = slice(block * BLK, (block + 1) * BLK)
        return normed * cos[place, :] + other * sin[place, :]

    for block in range(CAP // BLK):
        place = slice(block * BLK, (block + 1) * BLK)
        values = rows_in[place, :].astype(F32)
        center = values - jnp.mean(values, axis=1, keepdims=True)
        variance = jnp.mean(center * center, axis=1, keepdims=True)
        normed = center * lax.rsqrt(variance + 1e-05)
        token = piece * CAP + block * BLK + lax.broadcasted_iota(jnp.int32, (BLK, 1), 0)
        second = token >= boundary
        text = token - jnp.where(second, boundary, 0) < TEXT

        def pick(part):
            video_cols = slice(part * D, (part + 1) * D)
            text_cols = slice((part + 3) * D, (part + 4) * D)
            video_pick = jnp.where(second, mods[1:2, video_cols], mods[0:1, video_cols])
            text_pick = jnp.where(second, mods[1:2, text_cols], mods[0:1, text_cols])
            return jnp.where(text, text_pick, video_pick)

        modded = (normed * (1.0 + pick(1)) + pick(0)).astype(BF16)
        query = jnp.dot(modded, wq[...], preferred_element_type=F32)
        key = jnp.dot(modded, wk[...], preferred_element_type=F32)
        value = jnp.dot(modded, wv[...], preferred_element_type=F32)
        base = block * 192
        for group in range(3):
            cols = slice(group * 128, (group + 1) * 128)
            q_turn = head_prepare(query[:, cols], gq, block).T.astype(BF16)
            v_turn = value[:, cols].T.astype(BF16)
            k_rows = head_prepare(key[:, cols], gk, block)
            if group == 0:
                qa[base : base + 128, :] = q_turn
                kva[960 + base : 960 + base + 128, :] = v_turn
                kva[place, :] = k_rows.astype(BF16)
            elif group == 1:
                qa[base + 128 : base + 192, :] = q_turn[:64]
                qb[base + 128 : base + 192, :] = q_turn[64:]
                kva[960 + base + 128 : 960 + base + 192, :] = v_turn[:64]
                kvb[960 + base + 128 : 960 + base + 192, :] = v_turn[64:]
                middle[place, :] = k_rows
            else:
                qb[base : base + 128, :] = q_turn
                kvb[960 + base : 960 + base + 128, :] = v_turn
                kvb[place, :] = k_rows.astype(BF16)
    left = lax.broadcasted_iota(jnp.int32, (CAP // 2, 2 * HD), 1) < HD
    upper = middle[: CAP // 2, :]
    lower = middle[CAP // 2 :, :]
    kva[CAP:960, :] = jnp.where(left, upper, pltpu.roll(lower, HD, 1)).astype(BF16)
    kvb[CAP:960, :] = jnp.where(left, pltpu.roll(upper, HD, 1), lower).astype(BF16)


def project(info, chunks, mods, wq, wk, wv, cos, sin, gq, gk):
    vmem = pl.BlockSpec(memory_space=pltpu.VMEM)
    return pl.pallas_call(
        project_kernel,
        out_shape=[jax.ShapeDtypeStruct((2880, 128), BF16)] * 2,
        in_specs=[pl.BlockSpec(memory_space=pltpu.SMEM)] + [vmem] * 16,
        out_specs=[vmem] * 2,
        scratch_shapes=[pltpu.VMEM((CAP, D), BF16), pltpu.VMEM((CAP, 128), F32)],
        compiler_params=pltpu.CompilerParams(vmem_limit_bytes=VMEM_LIMIT),
        name="project",
    )(info, *chunks, mods, wq, wk, wv, cos, sin, gq, gk)


def attend_kernel(limits, *refs, places, near, carried, last):
    n_q, n_k = len(places), 3 if near else 4
    queries, refs = refs[:n_q], refs[n_q:]
    keys, refs = refs[:n_k], refs[n_k:]
    queries = [ref.at[:960] for ref in queries]
    keys = [ref.at[960:] for ref in keys]
    if carried:
        before, refs = refs[0], refs[1:]
    n_out = n_q if last else 1
    outs, refs = refs[:n_out], refs[n_out:]
    qs, ks, vs, todo = refs[:4]
    acc = refs[4] if last else outs[0]
    scale = math.log2(math.e) / math.sqrt(HD)
    line = lax.broadcasted_iota(jnp.int32, (CAP, 128), 0)
    lane = lax.broadcasted_iota(jnp.int32, (CAP, 128), 1)
    sub = lane % HD
    q_line = lax.broadcasted_iota(jnp.int32, (HD, CAP), 0)
    q_lane = lax.broadcasted_iota(jnp.int32, (HD, CAP), 1)
    ones = jnp.where(lax.broadcasted_iota(jnp.int32, (16, CAP), 0) == 0, 1.0, 0.0).astype(BF16)
    left = lane < HD

    kinds = [
        jnp.where(limits[4 + tile] == CAP, 0, jnp.where(limits[4 + tile] == 0, 2, 1))
        for tile in range(n_k)
    ]
    slots = []
    only_first = jnp.int32(0)
    only_second = jnp.int32(0)
    for tile in range(n_k):
        slot = jnp.int32(0)
        for other in range(n_k):
            if other < tile:
                slot = slot + jnp.where(kinds[other] <= kinds[tile], 1, 0)
            elif other > tile:
                slot = slot + jnp.where(kinds[other] < kinds[tile], 1, 0)
        slots.append(slot)
        only_first = only_first + jnp.where(kinds[tile] == 0, 1, 0)
        only_second = only_second + jnp.where(kinds[tile] == 2, 1, 0)
    for i, place in enumerate(places):
        has_first = limits[place] > 0
        has_second = limits[place] < CAP
        if carried and place != 3:
            shared = (has_first & (limits[7] > 0)) | (has_second & (limits[7] < CAP))
            todo[i] = slots[3]
            todo[8 + i] = jnp.where(shared, 1, 0)
        else:
            low = jnp.where(has_first, 0, only_first)
            todo[i] = low
            todo[8 + i] = jnp.where(has_second, n_k, n_k - only_second) - low

    for tile in range(n_k):
        start = pl.multiple_of(slots[tile] * CAP, 128)
        second = line >= limits[4 + tile]
        mark = jnp.where(
            sub == 0,
            jnp.where(second, BIG, 0.0),
            jnp.where(sub == 1, jnp.where(second, 0.0, BIG), 0.0),
        ).astype(BF16)
        pair = keys[tile][:CAP, :]
        ks[0, pl.ds(start, CAP), :] = jnp.where(left, pair, mark)
        ks[1, pl.ds(start, CAP), :] = jnp.where(left, mark, pair)
        end = keys[tile][CAP:960, :]
        half = CAP // 2
        turned = jnp.concatenate([end[:, HD:], end[:, :HD]], axis=1)
        ks[2, pl.ds(start, half), :] = jnp.where(left[:half], end, mark[:half])
        ks[2, pl.ds(start + half, half), :] = jnp.where(left[:half], turned, mark[half:])
        for head in range(3):
            vs[head, HD:, pl.ds(start, CAP)] = ones
            for block in range(5):
                v_row = 960 + 192 * block + HD * head
                vs[head, :HD, pl.ds(start + 128 * block, 128)] = keys[tile][v_row : v_row + HD, :]
    for i, place in enumerate(places):
        q_second = q_lane >= limits[place]
        q_mark = jnp.where(
            q_line == 0,
            jnp.where(q_second, 0.0, -1.0),
            jnp.where(q_line == 1, jnp.where(q_second, -1.0, 0.0), 0.0),
        ).astype(BF16)
        for head in range(3):
            at = HD if head == 1 else 0
            qs[i, head, HD - at : 2 * HD - at, :] = q_mark
            for block in range(5):
                row = 192 * block + HD * head
                cols = slice(128 * block, 128 * block + 128)
                qs[i, head, at : at + HD, cols] = queries[i][row : row + HD, :]
        if carried and place != 3:
            acc[i] = before[i]
        else:
            acc[i] = jnp.zeros((3, 80, CAP), F32)

    def part(i, head, start, count):
        scores = jnp.dot(
            ks[head, pl.ds(start, count), :], qs[i, head], preferred_element_type=F32
        )
        weights = jnp.exp2(scores * scale).astype(BF16)
        acc[i, head] += jnp.dot(
            vs[head, :, pl.ds(start, count)], weights, preferred_element_type=F32
        )

    def q_tile(i, carry):
        low = todo[i]
        count = todo[8 + i]

        def two(step, inner):
            start = pl.multiple_of((low + 2 * step) * CAP, 128)

            def one_head(head, rest):
                part(i, head, start, 2 * CAP)
                return rest

            return lax.fori_loop(0, 3, one_head, inner)

        lax.fori_loop(0, count // 2, two, 0)

        @pl.when(count % 2 == 1)
        def _():
            start = pl.multiple_of((low + count - 1) * CAP, 128)

            def one_head(head, rest):
                part(i, head, start, CAP)
                return rest

            lax.fori_loop(0, 3, one_head, 0)

        return carry

    lax.fori_loop(0, n_q, q_tile, 0)
    if last:
        for i, ref in enumerate(outs):
            sums = jnp.concatenate([acc[i, head, HD : HD + 1, :] for head in range(3)], axis=0)
            high = sums.astype(BF16)
            low = (sums - high.astype(F32)).astype(BF16)
            for head in range(3):
                ref[HD * head : HD * head + HD, :] = acc[i, head, :HD, :].astype(BF16)
            ref[192:195, :] = high
            ref[195:198, :] = low
            ref[198:208, :] = jnp.zeros((10, CAP), BF16)


def attend(limits, queries, keys, places, name, before=None):
    vmem = pl.BlockSpec(memory_space=pltpu.VMEM)
    n_q, n_k = len(places), len(keys)
    carried = before is not None
    if carried:
        out_shape = [jax.ShapeDtypeStruct((208, CAP), BF16)] * n_q
    else:
        out_shape = [jax.ShapeDtypeStruct((n_q, 3, 80, CAP), F32)]
    scratch = [
        pltpu.VMEM((n_q, 3, 128, CAP), BF16),
        pltpu.VMEM((3, n_k * CAP, 128), BF16),
        pltpu.VMEM((3, 80, n_k * CAP), BF16),
        pltpu.SMEM((16,), jnp.int32),
    ]
    if carried:
        scratch.append(pltpu.VMEM((n_q, 3, 80, CAP), F32))
    operands = [limits, *queries, *keys] + ([before] if carried else [])
    return pl.pallas_call(
        functools.partial(
            attend_kernel, places=places, near=n_k == 3, carried=carried, last=carried
        ),
        out_shape=out_shape,
        in_specs=[pl.BlockSpec(memory_space=pltpu.SMEM)] + [vmem] * (len(operands) - 1),
        out_specs=[vmem] * len(out_shape),
        scratch_shapes=scratch,
        cost_estimate=pl.CostEstimate(flops=1000, transcendentals=0, bytes_accessed=1000),
        compiler_params=pltpu.CompilerParams(vmem_limit_bytes=VMEM_LIMIT),
        name=name,
    )(*operands)


def merge_kernel(
    order, own_a, a1, a2, a3, own_b, b1, b2, b3, theirs, mine, turned, rows
):
    for own, others, heads in (
        (own_a, (a1, a2, a3), (0, 1, 2)),
        (own_b, (b1, b2, b3), (4, 5, 3)),
    ):
        for place, head in enumerate(heads):
            total = own[0, place, :HD, :]
            share = own[0, place, HD : HD + 1, :]
            for ref in others:
                total = total + ref[HD * place : HD * place + HD, :].astype(F32)
                tail = ref[192:208, :].astype(F32)
                share = share + tail[place : place + 1, :] + tail[3 + place : 4 + place, :]
            turned[HD * head : HD * head + HD, :] = total / share
    for block in range(5):
        place = slice(block * 128, block * 128 + 128)
        for group in range(3):
            cols = slice(group * 128, group * 128 + 128)
            rows[place, cols] = turned[cols, place].T.astype(BF16)
    for i in range(4):
        start = pl.multiple_of(order[i], 16)
        theirs[i * OWN : (i + 1) * OWN, :] = rows[pl.ds(start, OWN), :]
        start = pl.multiple_of(order[4 + i], 16)
        mine[i * OWN : (i + 1) * OWN, :] = rows[pl.ds(start, OWN), :]


def merge(order, own_a, others_a, own_b, others_b):
    vmem = pl.BlockSpec(memory_space=pltpu.VMEM)
    return pl.pallas_call(
        merge_kernel,
        out_shape=[jax.ShapeDtypeStruct((4 * OWN, 384), BF16)] * 2,
        in_specs=[pl.BlockSpec(memory_space=pltpu.SMEM)] + [vmem] * 8,
        out_specs=[vmem] * 2,
        scratch_shapes=[pltpu.VMEM((384, CAP), F32), pltpu.VMEM((CAP, 384), BF16)],
        compiler_params=pltpu.CompilerParams(vmem_limit_bytes=VMEM_LIMIT),
        name="merge",
    )(order, own_a, *others_a, own_b, *others_b)


def output_kernel(mine, theirs, w_here, w_other, own, out1, out2, out3):
    for i, ref in ((3, out3), (1, out1), (2, out2), (0, own)):
        rows = slice(i * OWN, (i + 1) * OWN)
        total = jnp.dot(mine[rows, :], w_here[...], preferred_element_type=F32)
        total += jnp.dot(theirs[rows, :], w_other[...], preferred_element_type=F32)
        ref[...] = total.astype(ref.dtype)


def output(mine, theirs, w_here, w_other):
    vmem = pl.BlockSpec(memory_space=pltpu.VMEM)
    return pl.pallas_call(
        output_kernel,
        out_shape=[jax.ShapeDtypeStruct((OWN, D), F32)]
        + [jax.ShapeDtypeStruct((OWN, D), BF16)] * 3,
        in_specs=[vmem] * 4,
        out_specs=[vmem] * 4,
        compiler_params=pltpu.CompilerParams(vmem_limit_bytes=VMEM_LIMIT),
        name="output",
    )(mine, theirs, w_here, w_other)


def select_gate(modulation, second, text):
    video_cols = modulation[:, 2 * D : 3 * D]
    text_cols = modulation[:, 5 * D : 6 * D]
    video_pick = jnp.where(second, video_cols[1][None, :], video_cols[0][None, :])
    text_pick = jnp.where(second, text_cols[1][None, :], text_cols[0][None, :])
    return jnp.where(text, text_pick, video_pick)


def local(
    tokens, w_query, w_key, w_value, w_out, w_mod, gain_query, gain_key, timesteps,
    video_lengths, piece_table,
):
    x, core = lax.axis_index("x"), lax.axis_index("core")
    z = lax.axis_index("z")
    y = lax.axis_index("yhi") * 2 + lax.axis_index("ylo")
    boundary = TEXT + video_lengths[0]

    across = [tokens] + [shift_x(tokens, step) for step in SHIFTS]
    chunks = across + [swap_core(chunk) for chunk in across]

    w_other = swap_core(w_out)

    act = jax.nn.silu(time_features(timesteps)).astype(BF16)
    part_mod = jnp.dot(act, w_mod, preferred_element_type=F32)
    width = part_mod.shape[1]
    packed = jnp.pad(part_mod.reshape(2 * width), (0, 384 - 2 * width)).reshape(3, 128)
    spread = lax.all_to_all(
        jnp.broadcast_to(packed[None], (128, 3, 128)), AXES, 0, 0, tiled=True
    ).reshape(128, 384)
    modulation = jnp.stack(
        [spread[:, :width].reshape(128 * width), spread[:, width : 2 * width].reshape(128 * width)]
    )

    back = jnp.array([0, 1, -1, 2], jnp.int32)
    z_ring = (z - back) % 4
    y_ring = (y - back) % 4
    z_tiles = ((y % 2) * 4 + z_ring) * 2 + y // 2
    y_tiles = ((y_ring % 2) * 4 + z) * 2 + y_ring // 2
    tiles = jnp.concatenate([z_tiles, y_tiles])
    pieces = jnp.sum(
        jnp.where(
            tiles[:, None] == jnp.arange(16, dtype=jnp.int32)[None, :], piece_table[None, :], 0
        ),
        axis=1,
    )
    limits_a = jnp.clip(boundary - pieces * CAP, 0, CAP)
    limits_b = jnp.concatenate([limits_a[4:], limits_a[:4]])
    piece = pieces[0]
    x_ring = (x - back) % 4
    starts = jnp.concatenate([(x_ring * 2 + core) * OWN, (x_ring * 2 + 1 - core) * OWN])
    info = jnp.concatenate([starts, jnp.stack([piece, boundary])])

    cos, sin = rope_tables(piece, boundary)
    gq = jnp.tile(gain_query, 2)[None, :]
    gk = jnp.tile(gain_key, 2)[None, :]
    along_z, along_y = project(
        info, chunks, modulation, w_query, w_key, w_value, cos, sin, gq, gk
    )
    from_z = [along_z] + [shift_z(along_z, step) for step in SHIFTS]
    from_y = [along_y] + [shift_y(along_y, step) for step in SHIFTS]
    near_a = attend(limits_a, from_z[1:3], from_y[:3], (1, 2), "near_a")[0]
    near_b = attend(limits_b, from_y[1:3], from_z[:3], (1, 2), "near_b")[0]
    limits_a, near_a, near_b = lax.optimization_barrier((limits_a, near_a, near_b))
    parts_a = attend(limits_a, from_z[1:], from_y, (1, 2, 3), "far_a", near_a)
    sent_a = [shift_z(part, -step) for part, step in zip(parts_a, SHIFTS)]
    limits_b, near_b, _ = lax.optimization_barrier((limits_b, near_b, parts_a[0]))
    parts_b = attend(limits_b, from_y[1:], from_z, (1, 2, 3), "far_b", near_b)
    sent_b = [shift_y(part, -step) for part, step in zip(parts_b, SHIFTS)]
    limits_a, limits_b, _ = lax.optimization_barrier((limits_a, limits_b, parts_b[0]))
    own_a = attend(limits_a, from_z[:1], from_y, (0,), "own_a")[0]
    own_b = attend(limits_b, from_y[:1], from_z, (0,), "own_b")[0]

    ahead = (x + back) % 4
    order = jnp.concatenate([(ahead * 2 + 1 - core) * OWN, (ahead * 2 + core) * OWN])
    theirs, mine = merge(order, own_a, sent_a, own_b, sent_b)
    received = swap_core(theirs)
    sums = output(mine, received, w_out, w_other)
    projection = sums[0]
    for share, step in zip(sums[1:], SHIFTS):
        projection = projection + shift_x(share, step).astype(F32)

    own_token = piece * CAP + starts[0] + jnp.arange(OWN, dtype=jnp.int32)[:, None]
    second = own_token >= boundary
    text = own_token - jnp.where(second, boundary, 0) < TEXT
    gate = select_gate(modulation, second, text)
    return (gate * projection).astype(BF16)


def solution(mesh):
    fine = Mesh(mesh.devices.reshape(2, 4, 2, 4, 2), AXES)
    tensor = ("x", "core")
    placed = (
        P(AXES, None),
        P(None, tensor),
        P(None, tensor),
        P(None, tensor),
        P(tensor, None),
        P(None, AXES),
        P(),
        P(),
        P(),
        P(),
        P(),
    )
    return jax.shard_map(
        local, mesh=fine, in_specs=placed, out_specs=P(AXES, None), check_vma=False
    )
```

```python
import functools
import math

import jax
import jax.numpy as jnp
from jax import lax
from jax.experimental import pallas as pl
from jax.experimental.pallas import tpu as pltpu
from jax.sharding import Mesh, PartitionSpec as P

HD = 64
TE = 512
TEXT = 226
HP = 30
WP = 45
CAP = 640
D = 3072
BLK = 128
OWN = 80
BIG = 16384.0
F32 = jnp.float32
BF16 = jnp.bfloat16

AXES = ("ylo", "z", "yhi", "x", "core")
Y_AXES = ("ylo", "yhi")
Y_INDEX = (0, 2, 1, 3)
VMEM_LIMIT = 60 * 1024 * 1024
SHIFTS = (1, -1, 2)


def shift_x(value, step):
    return lax.ppermute(value, "x", [(i, (i + step) % 4) for i in range(4)])


def shift_z(value, step):
    return lax.ppermute(value, "z", [(i, (i + step) % 4) for i in range(4)])


def shift_y(value, step):
    return lax.ppermute(value, Y_AXES, [(Y_INDEX[i], Y_INDEX[(i + step) % 4]) for i in range(4)])


def swap_core(value):
    return lax.ppermute(value, "core", [(0, 1), (1, 0)])


def time_features(timesteps):
    half_dim = TE // 2
    freqs = jnp.exp(-math.log(10000.0) * jnp.arange(half_dim, dtype=F32) / half_dim)
    angles = timesteps.astype(F32)[:, None] * freqs[None, :]
    return jnp.concatenate([jnp.cos(angles), jnp.sin(angles)], axis=1)


def rope_tables(piece, boundary):
    token = piece * CAP + lax.broadcasted_iota(jnp.int32, (CAP, 2 * HD), 0)
    lane = lax.broadcasted_iota(jnp.int32, (CAP, 2 * HD), 1)
    inner = token - jnp.where(token >= boundary, boundary, 0)
    is_text = inner < TEXT
    video = jnp.maximum(inner - TEXT, 0)
    frame = video // (HP * WP)
    height = video // WP % HP
    width = video % WP
    pair = lane % HD // 2
    time_pairs = HD // 8
    space_pairs = 3 * HD // 16
    freq_time = 10000.0 ** (-jnp.arange(0, HD // 4, 2, dtype=F32) / (HD // 4))
    freq_space = 10000.0 ** (-jnp.arange(0, 3 * HD // 8, 2, dtype=F32) / (3 * HD // 8))
    freq = jnp.concatenate([freq_time, freq_space, freq_space])
    freq = jnp.tile(jnp.repeat(freq, 2), 2)[None, :]
    place = jnp.where(
        pair < time_pairs, frame, jnp.where(pair < time_pairs + space_pairs, height, width)
    )
    angle = place.astype(F32) * freq
    cosine = jnp.where(is_text, 1.0, jnp.cos(angle))
    sine = jnp.where(is_text, 0.0, jnp.sin(angle))
    return cosine, jnp.where(lane % 2 == 0, -sine, sine)


def project_kernel(
    info, c0, c1, c2, c3, c4, c5, c6, c7, mods, wq_far, wk_far, wv_far, cos, sin, gq, gk,
    along_z, along_y, rows_in, wq, wk, wv, qa, kva, qb, kvb, middle, sems,
):
    copies = [
        pltpu.make_async_copy(source, target, sems.at[i])
        for i, (source, target) in enumerate(((wq_far, wq), (wk_far, wk), (wv_far, wv)))
    ]
    for copy in copies:
        copy.start()
    chunks = (c0, c1, c2, c3, c4, c5, c6, c7)
    for i, chunk in enumerate(chunks):
        rows_in[pl.ds(pl.multiple_of(info[i], 16), OWN), :] = chunk[...]
    piece = info[8]
    boundary = info[9]
    line = lax.broadcasted_iota(jnp.int32, (256, 128), 0)
    average = jnp.where(
        line % 128 // HD == lax.broadcasted_iota(jnp.int32, (256, 128), 1) // HD, 1.0 / HD, 0.0
    ).astype(BF16)
    even = lax.broadcasted_iota(jnp.int32, (BLK, 128), 1) % 2 == 0

    def head_mean(entries):
        high = entries.astype(BF16)
        low = (entries - high.astype(F32)).astype(BF16)
        return jnp.dot(
            jnp.concatenate([high, low], axis=1), average, preferred_element_type=F32
        )

    def head_prepare(entries, gain, block):
        center = entries - head_mean(entries)
        variance = head_mean(center * center)
        normed = center * lax.rsqrt(variance + 1e-06) * gain[...]
        other = jnp.where(even, pltpu.roll(normed, 127, 1), pltpu.roll(normed, 1, 1))
        place = slice(block * BLK, (block + 1) * BLK)
        return normed * cos[place, :] + other * sin[place, :]

    for block in range(CAP // BLK):
        place = slice(block * BLK, (block + 1) * BLK)
        values = rows_in[place, :].astype(F32)
        center = values - jnp.mean(values, axis=1, keepdims=True)
        variance = jnp.mean(center * center, axis=1, keepdims=True)
        normed = center * lax.rsqrt(variance + 1e-05)
        token = piece * CAP + block * BLK + lax.broadcasted_iota(jnp.int32, (BLK, 1), 0)
        second = token >= boundary
        text = token - jnp.where(second, boundary, 0) < TEXT

        def pick(part):
            video_cols = slice(part * D, (part + 1) * D)
            text_cols = slice((part + 3) * D, (part + 4) * D)
            video_pick = jnp.where(second, mods[1:2, video_cols], mods[0:1, video_cols])
            text_pick = jnp.where(second, mods[1:2, text_cols], mods[0:1, text_cols])
            return jnp.where(text, text_pick, video_pick)

        modded = (normed * (1.0 + pick(1)) + pick(0)).astype(BF16)
        if block == 0:
            for copy in copies:
                copy.wait()
        query = jnp.dot(modded, wq[...], preferred_element_type=F32)
        key = jnp.dot(modded, wk[...], preferred_element_type=F32)
        value = jnp.dot(modded, wv[...], preferred_element_type=F32)
        base = block * 192
        for group in range(3):
            cols = slice(group * 128, (group + 1) * 128)
            q_turn = head_prepare(query[:, cols], gq, block).T.astype(BF16)
            v_turn = value[:, cols].T.astype(BF16)
            k_rows = head_prepare(key[:, cols], gk, block)
            if group == 0:
                qa[base : base + 128, :] = q_turn
                kva[960 + base : 960 + base + 128, :] = v_turn
                kva[place, :] = k_rows.astype(BF16)
            elif group == 1:
                qa[base + 128 : base + 192, :] = q_turn[:64]
                qb[base + 128 : base + 192, :] = q_turn[64:]
                kva[960 + base + 128 : 960 + base + 192, :] = v_turn[:64]
                kvb[960 + base + 128 : 960 + base + 192, :] = v_turn[64:]
                middle[place, :] = k_rows
            else:
                qb[base : base + 128, :] = q_turn
                kvb[960 + base : 960 + base + 128, :] = v_turn
                kvb[place, :] = k_rows.astype(BF16)
    left = lax.broadcasted_iota(jnp.int32, (CAP // 2, 128), 1) < HD
    upper = middle[: CAP // 2, :]
    lower = middle[CAP // 2 :, :]
    kva[CAP:960, :] = jnp.where(left, upper, pltpu.roll(lower, HD, 1)).astype(BF16)
    kvb[CAP:960, :] = jnp.where(left, pltpu.roll(upper, HD, 1), lower).astype(BF16)
    along_z[:960, :] = qa[...]
    along_z[960:, :] = kvb[...]
    along_y[:960, :] = qb[...]
    along_y[960:, :] = kva[...]


def project(info, chunks, mods, wq, wk, wv, cos, sin, gq, gk):
    vmem = pl.BlockSpec(memory_space=pltpu.VMEM)
    return pl.pallas_call(
        project_kernel,
        out_shape=[jax.ShapeDtypeStruct((2880, 128), BF16)] * 2,
        in_specs=[pl.BlockSpec(memory_space=pltpu.SMEM)]
        + [vmem] * 9
        + [pl.BlockSpec(memory_space=pl.ANY)] * 3
        + [vmem] * 4,
        out_specs=[vmem] * 2,
        scratch_shapes=[pltpu.VMEM((CAP, D), BF16)]
        + [pltpu.VMEM((D, 384), BF16)] * 3
        + [pltpu.VMEM((960, 128), BF16), pltpu.VMEM((1920, 128), BF16)] * 2
        + [pltpu.VMEM((CAP, 128), F32), pltpu.SemaphoreType.DMA((3,))],
        compiler_params=pltpu.CompilerParams(vmem_limit_bytes=VMEM_LIMIT),
        name="project",
    )(info, *chunks, mods, wq, wk, wv, cos, sin, gq, gk)


def attend_kernel(limits, *refs, places, n_k, carried, last):
    n_q = len(places)
    queries, refs = refs[:n_q], refs[n_q:]
    keys, refs = refs[:n_k], refs[n_k:]
    if carried:
        before, refs = refs[0], refs[1:]
    n_out = n_q if last else 1
    outs, refs = refs[:n_out], refs[n_out:]
    qs, ks, vs, todo = refs[:4]
    acc = refs[4] if last else outs[0]
    scale = math.log2(math.e) / math.sqrt(HD)
    half = CAP // 2
    ones = jnp.where(lax.broadcasted_iota(jnp.int32, (16, CAP), 0) == 0, 1.0, 0.0).astype(BF16)
    blank = jnp.zeros((HD, CAP), BF16)

    kinds = [
        jnp.where(limits[4 + tile] == CAP, 0, jnp.where(limits[4 + tile] == 0, 2, 1))
        for tile in range(n_k)
    ]
    slots = []
    only_first = jnp.int32(0)
    only_second = jnp.int32(0)
    key_limit = jnp.int32(0)
    for tile in range(n_k):
        slot = jnp.int32(0)
        for other in range(n_k):
            if other < tile:
                slot = slot + jnp.where(kinds[other] <= kinds[tile], 1, 0)
            elif other > tile:
                slot = slot + jnp.where(kinds[other] < kinds[tile], 1, 0)
        slots.append(slot)
        only_first = only_first + jnp.where(kinds[tile] == 0, 1, 0)
        only_second = only_second + jnp.where(kinds[tile] == 2, 1, 0)
        key_limit = key_limit + limits[4 + tile]
    for i, place in enumerate(places):
        has_first = limits[place] > 0
        has_second = limits[place] < CAP
        todo[16 + i] = limits[place]
        if carried and place != 3:
            shared = (has_first & (limits[7] > 0)) | (has_second & (limits[7] < CAP))
            todo[i] = slots[3]
            todo[8 + i] = jnp.where(shared, 1, 0)
        else:
            low = jnp.where(has_first, 0, only_first)
            todo[i] = low
            todo[8 + i] = jnp.where(has_second, n_k, n_k - only_second) - low

    for tile in range(n_k):
        start = pl.multiple_of(slots[tile] * CAP, 64)
        ks[0, pl.ds(start, CAP), :] = keys[tile][:CAP, :]
        end = keys[tile][CAP:960, :]
        ks[1, pl.ds(start, half), :] = end
        ks[1, pl.ds(start + half, half), :] = jnp.concatenate([end[:, HD:], end[:, :HD]], axis=1)
        vs[pl.ds(pl.multiple_of(slots[tile] * 960, 64), 960), :] = keys[tile][960:, :]
    for i, place in enumerate(places):
        for head in range(3):
            at = HD if head == 1 else 0
            qs[i, head, HD - at : 2 * HD - at, :] = blank
            for block in range(5):
                row = 192 * block + HD * head
                cols = slice(128 * block, 128 * block + 128)
                qs[i, head, at : at + HD, cols] = queries[i][row : row + HD, :]
        if carried and place != 3:
            acc[i] = before[i]
        else:
            acc[i] = jnp.zeros((3, 80, CAP), F32)

    def part(i, head, slot, count, masked):
        first = pl.multiple_of(slot * CAP, 64)
        bank = jnp.where(head == 2, 1, 0)
        scores = jnp.dot(
            ks[bank, pl.ds(first, count * CAP), :], qs[i, head], preferred_element_type=F32
        )
        weights = jnp.exp2(scores * scale).astype(BF16)
        columns = []
        for block in range(5 * count):
            start = slot * 960 + head * HD + 192 * block
            columns.append(vs[pl.ds(pl.multiple_of(start, HD), HD), :])
        value = jnp.concatenate(
            [jnp.concatenate(columns, axis=1), jnp.concatenate([ones] * count, axis=1)], axis=0
        )
        place = first + lax.broadcasted_iota(jnp.int32, value.shape, 1)
        k_second = jnp.where(place >= key_limit, 1, 0)
        nothing = jnp.zeros_like(value)
        if masked:
            value = jnp.concatenate(
                [
                    jnp.where(k_second == 0, value, nothing),
                    jnp.where(k_second == 1, value, nothing),
                ],
                axis=0,
            )
            both = jnp.dot(value, weights, preferred_element_type=F32)
            q_second = lax.broadcasted_iota(jnp.int32, (80, CAP), 1) >= todo[16 + i]
            acc[i, head] += jnp.where(q_second, both[80:], both[:80])
        else:
            sample = jnp.where(todo[16 + i] > 0, 0, 1)
            value = jnp.where(k_second == sample, value, nothing)
            acc[i, head] += jnp.dot(value, weights, preferred_element_type=F32)

    def heads(i, slot, count):
        limit = todo[16 + i]
        mixed = (limit > 0) & (limit < CAP)
        for masked, test in ((False, jnp.logical_not(mixed)), (True, mixed)):

            @pl.when(test)
            def _():
                def one_head(head, rest):
                    part(i, head, slot, count, masked)
                    return rest

                lax.fori_loop(0, 3, one_head, 0)

    def q_tile(i, carry):
        low = todo[i]
        count = todo[8 + i]

        def two(step, inner):
            heads(i, low + 2 * step, 2)
            return inner

        lax.fori_loop(0, count // 2, two, 0)

        @pl.when(count % 2 == 1)
        def _():
            heads(i, low + count - 1, 1)

        return carry

    lax.fori_loop(0, n_q, q_tile, 0)
    if last:
        for i, (place, ref) in enumerate(zip(places, outs)):
            if place == 0:
                ref[...] = acc[i]
                continue
            sums = jnp.concatenate([acc[i, head, HD : HD + 1, :] for head in range(3)], axis=0)
            high = sums.astype(BF16)
            low = (sums - high.astype(F32)).astype(BF16)
            for head in range(3):
                ref[HD * head : HD * head + HD, :] = acc[i, head, :HD, :].astype(BF16)
            ref[192:195, :] = high
            ref[195:198, :] = low
            ref[198:208, :] = jnp.zeros((10, CAP), BF16)


def attend(limits, queries, keys, places, name, before=None):
    vmem = pl.BlockSpec(memory_space=pltpu.VMEM)
    n_q, n_k = len(places), len(keys)
    carried = before is not None
    last = n_k == 4
    if last:
        out_shape = [
            jax.ShapeDtypeStruct((208, CAP), BF16)
            if place
            else jax.ShapeDtypeStruct((3, 80, CAP), F32)
            for place in places
        ]
    else:
        out_shape = [jax.ShapeDtypeStruct((n_q, 3, 80, CAP), F32)]
    scratch = [
        pltpu.VMEM((n_q, 3, 128, CAP), BF16),
        pltpu.VMEM((2, n_k * CAP, 128), BF16),
        pltpu.VMEM((n_k * 960, 128), BF16),
        pltpu.SMEM((24,), jnp.int32),
    ]
    if last:
        scratch.append(pltpu.VMEM((n_q, 3, 80, CAP), F32))
    q_spec = pl.BlockSpec((960, 128), lambda i: (0, 0))
    k_spec = pl.BlockSpec((pl.Element(1920), pl.Element(128)), lambda i: (960, 0))
    operands = [limits, *queries, *keys] + ([before] if carried else [])
    specs = [pl.BlockSpec(memory_space=pltpu.SMEM)] + [q_spec] * n_q + [k_spec] * n_k
    return pl.pallas_call(
        functools.partial(attend_kernel, places=places, n_k=n_k, carried=carried, last=last),
        out_shape=out_shape,
        grid=(1,),
        in_specs=specs + [vmem] * (len(operands) - len(specs)),
        out_specs=[vmem] * len(out_shape),
        scratch_shapes=scratch,
        cost_estimate=pl.CostEstimate(flops=1000, transcendentals=0, bytes_accessed=1000),
        compiler_params=pltpu.CompilerParams(vmem_limit_bytes=VMEM_LIMIT),
        name=name,
    )(*operands)


def merge_kernel(
    order, own_a, a1, a2, a3, own_b, b1, b2, b3, theirs, mine, turned, rows
):
    for own, others, heads in (
        (own_a, (a1, a2, a3), (0, 1, 2)),
        (own_b, (b1, b2, b3), (4, 5, 3)),
    ):
        for place, head in enumerate(heads):
            total = own[place, :HD, :]
            share = own[place, HD : HD + 1, :]
            for ref in others:
                total = total + ref[HD * place : HD * place + HD, :].astype(F32)
                tail = ref[192:208, :].astype(F32)
                share = share + tail[place : place + 1, :] + tail[3 + place : 4 + place, :]
            turned[HD * head : HD * head + HD, :] = total / share
    for block in range(5):
        place = slice(block * 128, block * 128 + 128)
        for group in range(3):
            cols = slice(group * 128, group * 128 + 128)
            rows[place, cols] = turned[cols, place].T.astype(BF16)
    for i in range(4):
        start = pl.multiple_of(order[i], 16)
        theirs[i * OWN : (i + 1) * OWN, :] = rows[pl.ds(start, OWN), :]
        start = pl.multiple_of(order[4 + i], 16)
        mine[i * OWN : (i + 1) * OWN, :] = rows[pl.ds(start, OWN), :]


def merge(order, own_a, others_a, own_b, others_b):
    vmem = pl.BlockSpec(memory_space=pltpu.VMEM)
    return pl.pallas_call(
        merge_kernel,
        out_shape=[jax.ShapeDtypeStruct((4 * OWN, 384), BF16)] * 2,
        in_specs=[pl.BlockSpec(memory_space=pltpu.SMEM)] + [vmem] * 8,
        out_specs=[vmem] * 2,
        scratch_shapes=[pltpu.VMEM((384, CAP), F32), pltpu.VMEM((CAP, 384), BF16)],
        compiler_params=pltpu.CompilerParams(vmem_limit_bytes=VMEM_LIMIT),
        name="merge",
    )(order, own_a, *others_a, own_b, *others_b)


def output_kernel(mine, theirs, w_here, w_other, own, out1, out2, out3):
    for lo, hi in ((2, 4), (0, 2)):
        rows = slice(lo * OWN, hi * OWN)
        total = jnp.dot(mine[rows, :], w_here[...], preferred_element_type=F32)
        total += jnp.dot(theirs[rows, :], w_other[...], preferred_element_type=F32)
        for i in range(lo, hi):
            ref = (own, out1, out2, out3)[i]
            ref[...] = total[(i - lo) * OWN : (i - lo + 1) * OWN].astype(ref.dtype)


def output(mine, theirs, w_here, w_other):
    vmem = pl.BlockSpec(memory_space=pltpu.VMEM)
    return pl.pallas_call(
        output_kernel,
        out_shape=[jax.ShapeDtypeStruct((OWN, D), F32)]
        + [jax.ShapeDtypeStruct((OWN, D), BF16)] * 3,
        in_specs=[vmem] * 4,
        out_specs=[vmem] * 4,
        compiler_params=pltpu.CompilerParams(vmem_limit_bytes=VMEM_LIMIT),
        name="output",
    )(mine, theirs, w_here, w_other)


def select_gate(modulation, second, text):
    video_cols = modulation[:, 2 * D : 3 * D]
    text_cols = modulation[:, 5 * D : 6 * D]
    video_pick = jnp.where(second, video_cols[1][None, :], video_cols[0][None, :])
    text_pick = jnp.where(second, text_cols[1][None, :], text_cols[0][None, :])
    return jnp.where(text, text_pick, video_pick)


def local(
    tokens, w_query, w_key, w_value, w_out, w_mod, gain_query, gain_key, timesteps,
    video_lengths, piece_table,
):
    x, core = lax.axis_index("x"), lax.axis_index("core")
    z = lax.axis_index("z")
    y = lax.axis_index("yhi") * 2 + lax.axis_index("ylo")
    boundary = TEXT + video_lengths[0]

    across = [tokens] + [shift_x(tokens, step) for step in SHIFTS]
    chunks = across + [swap_core(chunk) for chunk in across]

    w_other = swap_core(w_out)

    act = jax.nn.silu(time_features(timesteps)).astype(BF16)
    part_mod = jnp.dot(act, w_mod, preferred_element_type=F32)
    width = part_mod.shape[1]
    packed = jnp.pad(part_mod.reshape(2 * width), (0, 384 - 2 * width)).reshape(3, 128)
    spread = lax.all_to_all(
        jnp.broadcast_to(packed[None], (128, 3, 128)), AXES, 0, 0, tiled=True
    ).reshape(128, 384)
    modulation = jnp.stack(
        [spread[:, :width].reshape(128 * width), spread[:, width : 2 * width].reshape(128 * width)]
    )

    back = jnp.array([0, 1, -1, 2], jnp.int32)
    z_ring = (z - back) % 4
    y_ring = (y - back) % 4
    z_tiles = ((y % 2) * 4 + z_ring) * 2 + y // 2
    y_tiles = ((y_ring % 2) * 4 + z) * 2 + y_ring // 2
    tiles = jnp.concatenate([z_tiles, y_tiles])
    pieces = jnp.sum(
        jnp.where(
            tiles[:, None] == jnp.arange(16, dtype=jnp.int32)[None, :], piece_table[None, :], 0
        ),
        axis=1,
    )
    limits_a = jnp.clip(boundary - pieces * CAP, 0, CAP)
    limits_b = jnp.concatenate([limits_a[4:], limits_a[:4]])
    piece = pieces[0]
    x_ring = (x - back) % 4
    starts = jnp.concatenate([(x_ring * 2 + core) * OWN, (x_ring * 2 + 1 - core) * OWN])
    info = jnp.concatenate([starts, jnp.stack([piece, boundary])])

    cos, sin = rope_tables(piece, boundary)
    gq = jnp.tile(gain_query, 2)[None, :]
    gk = jnp.tile(gain_key, 2)[None, :]
    along_z, along_y = project(
        info, chunks, modulation, w_query, w_key, w_value, cos, sin, gq, gk
    )
    from_z = [along_z] + [shift_z(along_z, step) for step in SHIFTS]
    from_y = [along_y] + [shift_y(along_y, step) for step in SHIFTS]
    near_a = attend(limits_a, from_z[:3], from_y[:3], (0, 1, 2), "near_a")[0]
    own_a, *parts_a = attend(limits_a, from_z, from_y, (0, 1, 2, 3), "far_a", near_a)
    sent_a = [shift_z(part, -step) for part, step in zip(parts_a, SHIFTS)]
    limits_b, _ = lax.optimization_barrier((limits_b, parts_a[0]))
    parts_b = attend(limits_b, from_y[1:], from_z, (1, 2, 3), "rest_b")
    sent_b = [shift_y(part, -step) for part, step in zip(parts_b, SHIFTS)]
    limits_b, _ = lax.optimization_barrier((limits_b, (parts_b[0], sent_a)))
    own_b = attend(limits_b, from_y[:1], from_z, (0,), "own_b")[0]

    ahead = (x + back) % 4
    order = jnp.concatenate([(ahead * 2 + 1 - core) * OWN, (ahead * 2 + core) * OWN])
    theirs, mine = merge(order, own_a, sent_a, own_b, sent_b)
    received = swap_core(theirs)
    sums = output(mine, received, w_out, w_other)
    projection = sums[0]
    for share, step in zip(sums[1:], SHIFTS):
        projection = projection + shift_x(share, step).astype(F32)

    own_token = piece * CAP + starts[0] + jnp.arange(OWN, dtype=jnp.int32)[:, None]
    second = own_token >= boundary
    text = own_token - jnp.where(second, boundary, 0) < TEXT
    gate = select_gate(modulation, second, text)
    return (gate * projection).astype(BF16)


def solution(mesh):
    fine = Mesh(mesh.devices.reshape(2, 4, 2, 4, 2), AXES)
    tensor = ("x", "core")
    placed = (
        P(AXES, None),
        P(None, tensor),
        P(None, tensor),
        P(None, tensor),
        P(tensor, None),
        P(None, AXES),
        P(),
        P(),
        P(),
        P(),
        P(),
    )
    return jax.shard_map(
        local, mesh=fine, in_specs=placed, out_specs=P(AXES, None), check_vma=False
    )
```

```python
import functools
import math

import jax
import jax.numpy as jnp
from jax import lax
from jax.experimental import pallas as pl
from jax.experimental.pallas import tpu as pltpu
from jax.sharding import Mesh, PartitionSpec as P

HD = 64
TE = 512
TEXT = 226
HP = 30
WP = 45
CAP = 640
D = 3072
BLK = 128
OWN = 80
BIG = 16384.0
F32 = jnp.float32
BF16 = jnp.bfloat16

AXES = ("ylo", "z", "yhi", "x", "core")
Y_AXES = ("ylo", "yhi")
Y_INDEX = (0, 2, 1, 3)
VMEM_LIMIT = 60 * 1024 * 1024
SHIFTS = (1, -1, 2)


def shift_x(value, step):
    return lax.ppermute(value, "x", [(i, (i + step) % 4) for i in range(4)])


def shift_z(value, step):
    return lax.ppermute(value, "z", [(i, (i + step) % 4) for i in range(4)])


def shift_y(value, step):
    return lax.ppermute(value, Y_AXES, [(Y_INDEX[i], Y_INDEX[(i + step) % 4]) for i in range(4)])


def swap_core(value):
    return lax.ppermute(value, "core", [(0, 1), (1, 0)])


def time_features(timesteps):
    half_dim = TE // 2
    freqs = jnp.exp(-math.log(10000.0) * jnp.arange(half_dim, dtype=F32) / half_dim)
    angles = timesteps.astype(F32)[:, None] * freqs[None, :]
    return jnp.concatenate([jnp.cos(angles), jnp.sin(angles)], axis=1)


def rope_tables(piece, boundary):
    token = piece * CAP + lax.broadcasted_iota(jnp.int32, (CAP, 2 * HD), 0)
    lane = lax.broadcasted_iota(jnp.int32, (CAP, 2 * HD), 1)
    inner = token - jnp.where(token >= boundary, boundary, 0)
    is_text = inner < TEXT
    video = jnp.maximum(inner - TEXT, 0)
    frame = video // (HP * WP)
    height = video // WP % HP
    width = video % WP
    pair = lane % HD // 2
    time_pairs = HD // 8
    space_pairs = 3 * HD // 16
    freq_time = 10000.0 ** (-jnp.arange(0, HD // 4, 2, dtype=F32) / (HD // 4))
    freq_space = 10000.0 ** (-jnp.arange(0, 3 * HD // 8, 2, dtype=F32) / (3 * HD // 8))
    freq = jnp.concatenate([freq_time, freq_space, freq_space])
    freq = jnp.tile(jnp.repeat(freq, 2), 2)[None, :]
    place = jnp.where(
        pair < time_pairs, frame, jnp.where(pair < time_pairs + space_pairs, height, width)
    )
    angle = place.astype(F32) * freq
    cosine = jnp.where(is_text, 1.0, jnp.cos(angle))
    sine = jnp.where(is_text, 0.0, jnp.sin(angle))
    return cosine, jnp.where(lane % 2 == 0, -sine, sine)


def project_kernel(
    info, c0, c1, c2, c3, c4, c5, c6, c7, mods, wq_far, wk_far, wv_far, cos, sin, gq, gk,
    along_z, along_y, rows_in, wq, wk, wv, qa, kva, qb, kvb, middle, sems,
):
    copies = [
        pltpu.make_async_copy(source, target, sems.at[i])
        for i, (source, target) in enumerate(((wq_far, wq), (wk_far, wk), (wv_far, wv)))
    ]
    for copy in copies:
        copy.start()
    chunks = (c0, c1, c2, c3, c4, c5, c6, c7)
    gain_q = jnp.concatenate([gq[...], gq[...]], axis=1)
    gain_k = jnp.concatenate([gk[...], gk[...]], axis=1)
    for i, chunk in enumerate(chunks):
        rows_in[pl.ds(pl.multiple_of(info[i], 16), OWN), :] = chunk[...]
    piece = info[8]
    boundary = info[9]
    line = lax.broadcasted_iota(jnp.int32, (256, 128), 0)
    average = jnp.where(
        line % 128 // HD == lax.broadcasted_iota(jnp.int32, (256, 128), 1) // HD, 1.0 / HD, 0.0
    ).astype(BF16)
    even = lax.broadcasted_iota(jnp.int32, (BLK, 128), 1) % 2 == 0

    def head_mean(entries):
        high = entries.astype(BF16)
        low = (entries - high.astype(F32)).astype(BF16)
        return jnp.dot(
            jnp.concatenate([high, low], axis=1), average, preferred_element_type=F32
        )

    def head_prepare(entries, gain, block):
        center = entries - head_mean(entries)
        variance = head_mean(center * center)
        normed = center * lax.rsqrt(variance + 1e-06) * gain
        other = jnp.where(even, pltpu.roll(normed, 127, 1), pltpu.roll(normed, 1, 1))
        place = slice(block * BLK, (block + 1) * BLK)
        return normed * cos[place, :] + other * sin[place, :]

    for block in range(CAP // BLK):
        place = slice(block * BLK, (block + 1) * BLK)
        values = rows_in[place, :].astype(F32)
        center = values - jnp.mean(values, axis=1, keepdims=True)
        variance = jnp.mean(center * center, axis=1, keepdims=True)
        normed = center * lax.rsqrt(variance + 1e-05)
        token = piece * CAP + block * BLK + lax.broadcasted_iota(jnp.int32, (BLK, 1), 0)
        second = token >= boundary
        text = token - jnp.where(second, boundary, 0) < TEXT

        def pick(part):
            video_cols = slice(part * D, (part + 1) * D)
            text_cols = slice((part + 3) * D, (part + 4) * D)
            video_pick = jnp.where(second, mods[1:2, video_cols], mods[0:1, video_cols])
            text_pick = jnp.where(second, mods[1:2, text_cols], mods[0:1, text_cols])
            return jnp.where(text, text_pick, video_pick)

        modded = (normed * (1.0 + pick(1)) + pick(0)).astype(BF16)
        if block == 0:
            for copy in copies:
                copy.wait()
        query = jnp.dot(modded, wq[...], preferred_element_type=F32)
        key = jnp.dot(modded, wk[...], preferred_element_type=F32)
        value = jnp.dot(modded, wv[...], preferred_element_type=F32)
        base = block * 192
        for group in range(3):
            cols = slice(group * 128, (group + 1) * 128)
            q_turn = head_prepare(query[:, cols], gain_q, block).T.astype(BF16)
            v_turn = value[:, cols].T.astype(BF16)
            k_rows = head_prepare(key[:, cols], gain_k, block)
            if group == 0:
                qa[base : base + 128, :] = q_turn
                kva[960 + base : 960 + base + 128, :] = v_turn
                kva[place, :] = k_rows.astype(BF16)
            elif group == 1:
                qa[base + 128 : base + 192, :] = q_turn[:64]
                qb[base + 128 : base + 192, :] = q_turn[64:]
                kva[960 + base + 128 : 960 + base + 192, :] = v_turn[:64]
                kvb[960 + base + 128 : 960 + base + 192, :] = v_turn[64:]
                middle[place, :] = k_rows
            else:
                qb[base : base + 128, :] = q_turn
                kvb[960 + base : 960 + base + 128, :] = v_turn
                kvb[place, :] = k_rows.astype(BF16)
    left = lax.broadcasted_iota(jnp.int32, (CAP // 2, 128), 1) < HD
    upper = middle[: CAP // 2, :]
    lower = middle[CAP // 2 :, :]
    kva[CAP:960, :] = jnp.where(left, upper, pltpu.roll(lower, HD, 1)).astype(BF16)
    kvb[CAP:960, :] = jnp.where(left, pltpu.roll(upper, HD, 1), lower).astype(BF16)
    along_z[:960, :] = qa[...]
    along_z[960:, :] = kvb[...]
    along_y[:960, :] = qb[...]
    along_y[960:, :] = kva[...]


def project(info, chunks, mods, wq, wk, wv, cos, sin, gq, gk):
    vmem = pl.BlockSpec(memory_space=pltpu.VMEM)
    return pl.pallas_call(
        project_kernel,
        out_shape=[jax.ShapeDtypeStruct((2880, 128), BF16)] * 2,
        in_specs=[pl.BlockSpec(memory_space=pltpu.SMEM)]
        + [vmem] * 9
        + [pl.BlockSpec(memory_space=pl.ANY)] * 3
        + [vmem] * 4,
        out_specs=[vmem] * 2,
        scratch_shapes=[pltpu.VMEM((CAP, D), BF16)]
        + [pltpu.VMEM((D, 384), BF16)] * 3
        + [pltpu.VMEM((960, 128), BF16), pltpu.VMEM((1920, 128), BF16)] * 2
        + [pltpu.VMEM((CAP, 128), F32), pltpu.SemaphoreType.DMA((3,))],
        compiler_params=pltpu.CompilerParams(vmem_limit_bytes=VMEM_LIMIT),
        name="project",
    )(info, *chunks, mods, wq, wk, wv, cos, sin, gq, gk)


def attend_kernel(limits, *refs, places, n_k, carried, last):
    n_q = len(places)
    queries, refs = refs[:n_q], refs[n_q:]
    keys, refs = refs[:n_k], refs[n_k:]
    if carried:
        before, refs = refs[0], refs[1:]
    n_out = n_q if last else 1
    outs, refs = refs[:n_out], refs[n_out:]
    qs, ks, vs, todo = refs[:4]
    acc = refs[4] if last else outs[0]
    scale = math.log2(math.e) / math.sqrt(HD)
    half = CAP // 2
    ones = jnp.where(lax.broadcasted_iota(jnp.int32, (16, CAP), 0) == 0, 1.0, 0.0).astype(BF16)
    blank = jnp.zeros((HD, CAP), BF16)

    kinds = [
        jnp.where(limits[4 + tile] == CAP, 0, jnp.where(limits[4 + tile] == 0, 2, 1))
        for tile in range(n_k)
    ]
    slots = []
    only_first = jnp.int32(0)
    only_second = jnp.int32(0)
    key_limit = jnp.int32(0)
    for tile in range(n_k):
        slot = jnp.int32(0)
        for other in range(n_k):
            if other < tile:
                slot = slot + jnp.where(kinds[other] <= kinds[tile], 1, 0)
            elif other > tile:
                slot = slot + jnp.where(kinds[other] < kinds[tile], 1, 0)
        slots.append(slot)
        only_first = only_first + jnp.where(kinds[tile] == 0, 1, 0)
        only_second = only_second + jnp.where(kinds[tile] == 2, 1, 0)
        key_limit = key_limit + limits[4 + tile]
    for i, place in enumerate(places):
        has_first = limits[place] > 0
        has_second = limits[place] < CAP
        todo[16 + i] = limits[place]
        if carried and place != 3:
            shared = (has_first & (limits[7] > 0)) | (has_second & (limits[7] < CAP))
            todo[i] = slots[3]
            todo[8 + i] = jnp.where(shared, 1, 0)
        else:
            low = jnp.where(has_first, 0, only_first)
            todo[i] = low
            todo[8 + i] = jnp.where(has_second, n_k, n_k - only_second) - low

    for tile in range(n_k):
        start = pl.multiple_of(slots[tile] * CAP, 64)
        ks[0, pl.ds(start, CAP), :] = keys[tile][:CAP, :]
        end = keys[tile][CAP:960, :]
        ks[1, pl.ds(start, half), :] = end
        ks[1, pl.ds(start + half, half), :] = jnp.concatenate([end[:, HD:], end[:, :HD]], axis=1)
        vs[pl.ds(pl.multiple_of(slots[tile] * 960, 64), 960), :] = keys[tile][960:, :]
    for i, place in enumerate(places):
        for head in range(3):
            at = HD if head == 1 else 0
            qs[i, head, HD - at : 2 * HD - at, :] = blank
            for block in range(5):
                row = 192 * block + HD * head
                cols = slice(128 * block, 128 * block + 128)
                qs[i, head, at : at + HD, cols] = queries[i][row : row + HD, :]
        if carried and place != 3:
            acc[i] = before[i]
        else:
            acc[i] = jnp.zeros((3, 80, CAP), F32)

    def part(i, head, slot, count, masked):
        first = pl.multiple_of(slot * CAP, 64)
        bank = jnp.where(head == 2, 1, 0)
        scores = jnp.dot(
            ks[bank, pl.ds(first, count * CAP), :], qs[i, head], preferred_element_type=F32
        )
        weights = jnp.exp2(scores * scale).astype(BF16)
        columns = []
        for block in range(5 * count):
            start = slot * 960 + head * HD + 192 * block
            columns.append(vs[pl.ds(pl.multiple_of(start, HD), HD), :])
        value = jnp.concatenate(
            [jnp.concatenate(columns, axis=1), jnp.concatenate([ones] * count, axis=1)], axis=0
        )
        place = first + lax.broadcasted_iota(jnp.int32, value.shape, 1)
        k_second = jnp.where(place >= key_limit, 1, 0)
        nothing = jnp.zeros_like(value)
        if masked:
            value = jnp.concatenate(
                [
                    jnp.where(k_second == 0, value, nothing),
                    jnp.where(k_second == 1, value, nothing),
                ],
                axis=0,
            )
            both = jnp.dot(value, weights, preferred_element_type=F32)
            q_second = lax.broadcasted_iota(jnp.int32, (80, CAP), 1) >= todo[16 + i]
            acc[i, head] += jnp.where(q_second, both[80:], both[:80])
        else:
            sample = jnp.where(todo[16 + i] > 0, 0, 1)
            value = jnp.where(k_second == sample, value, nothing)
            acc[i, head] += jnp.dot(value, weights, preferred_element_type=F32)

    def heads(i, slot, count, masked):
        def one_head(head, rest):
            part(i, head, slot, count, masked)
            return rest

        lax.fori_loop(0, 3, one_head, 0)

    def q_tile(i, carry):
        low = todo[i]
        count = todo[8 + i]
        limit = todo[16 + i]
        mixed = (limit > 0) & (limit < CAP)

        @pl.when(mixed)
        def _():
            def one(step, inner):
                heads(i, low + step, 1, True)
                return inner

            lax.fori_loop(0, count, one, 0)

        @pl.when(jnp.logical_not(mixed))
        def _():
            def two(step, inner):
                heads(i, low + 2 * step, 2, False)
                return inner

            lax.fori_loop(0, count // 2, two, 0)

            @pl.when(count % 2 == 1)
            def _():
                heads(i, low + count - 1, 1, False)

        return carry

    lax.fori_loop(0, n_q, q_tile, 0)
    if last:
        for i, (place, ref) in enumerate(zip(places, outs)):
            if place == 0:
                ref[...] = acc[i]
                continue
            sums = jnp.concatenate([acc[i, head, HD : HD + 1, :] for head in range(3)], axis=0)
            high = sums.astype(BF16)
            low = (sums - high.astype(F32)).astype(BF16)
            for head in range(3):
                ref[HD * head : HD * head + HD, :] = acc[i, head, :HD, :].astype(BF16)
            ref[192:195, :] = high
            ref[195:198, :] = low
            ref[198:208, :] = jnp.zeros((10, CAP), BF16)


def attend(limits, queries, keys, places, name, before=None):
    vmem = pl.BlockSpec(memory_space=pltpu.VMEM)
    n_q, n_k = len(places), len(keys)
    carried = before is not None
    last = n_k == 4
    if last:
        out_shape = [
            jax.ShapeDtypeStruct((208, CAP), BF16)
            if place
            else jax.ShapeDtypeStruct((3, 80, CAP), F32)
            for place in places
        ]
    else:
        out_shape = [jax.ShapeDtypeStruct((n_q, 3, 80, CAP), F32)]
    scratch = [
        pltpu.VMEM((n_q, 3, 128, CAP), BF16),
        pltpu.VMEM((2, n_k * CAP, 128), BF16),
        pltpu.VMEM((n_k * 960, 128), BF16),
        pltpu.SMEM((24,), jnp.int32),
    ]
    if last:
        scratch.append(pltpu.VMEM((n_q, 3, 80, CAP), F32))
    q_spec = pl.BlockSpec((960, 128), lambda i: (0, 0))
    k_spec = pl.BlockSpec((pl.Element(1920), pl.Element(128)), lambda i: (960, 0))
    operands = [limits, *queries, *keys] + ([before] if carried else [])
    specs = [pl.BlockSpec(memory_space=pltpu.SMEM)] + [q_spec] * n_q + [k_spec] * n_k
    return pl.pallas_call(
        functools.partial(attend_kernel, places=places, n_k=n_k, carried=carried, last=last),
        out_shape=out_shape,
        grid=(1,),
        in_specs=specs + [vmem] * (len(operands) - len(specs)),
        out_specs=[vmem] * len(out_shape),
        scratch_shapes=scratch,
        cost_estimate=pl.CostEstimate(flops=1000, transcendentals=0, bytes_accessed=1000),
        compiler_params=pltpu.CompilerParams(vmem_limit_bytes=VMEM_LIMIT),
        name=name,
    )(*operands)


def merge_kernel(
    order, own_a, a1, a2, a3, own_b, b1, b2, b3, theirs, mine, turned, rows
):
    for own, others, heads in (
        (own_a, (a1, a2, a3), (0, 1, 2)),
        (own_b, (b1, b2, b3), (4, 5, 3)),
    ):
        for place, head in enumerate(heads):
            total = own[place, :HD, :]
            share = own[place, HD : HD + 1, :]
            for ref in others:
                total = total + ref[HD * place : HD * place + HD, :].astype(F32)
                tail = ref[192:208, :].astype(F32)
                share = share + tail[place : place + 1, :] + tail[3 + place : 4 + place, :]
            turned[HD * head : HD * head + HD, :] = total / share
    for block in range(5):
        place = slice(block * 128, block * 128 + 128)
        for group in range(3):
            cols = slice(group * 128, group * 128 + 128)
            rows[place, cols] = turned[cols, place].T.astype(BF16)
    for i in range(4):
        start = pl.multiple_of(order[i], 16)
        theirs[i * OWN : (i + 1) * OWN, :] = rows[pl.ds(start, OWN), :]
        start = pl.multiple_of(order[4 + i], 16)
        mine[i * OWN : (i + 1) * OWN, :] = rows[pl.ds(start, OWN), :]


def merge(order, own_a, others_a, own_b, others_b):
    vmem = pl.BlockSpec(memory_space=pltpu.VMEM)
    return pl.pallas_call(
        merge_kernel,
        out_shape=[jax.ShapeDtypeStruct((4 * OWN, 384), BF16)] * 2,
        in_specs=[pl.BlockSpec(memory_space=pltpu.SMEM)] + [vmem] * 8,
        out_specs=[vmem] * 2,
        scratch_shapes=[pltpu.VMEM((384, CAP), F32), pltpu.VMEM((CAP, 384), BF16)],
        compiler_params=pltpu.CompilerParams(vmem_limit_bytes=VMEM_LIMIT),
        name="merge",
    )(order, own_a, *others_a, own_b, *others_b)


def output_kernel(mine, theirs, w_here, w_other, own, out1, out2, out3):
    for lo, hi in ((2, 4), (0, 2)):
        rows = slice(lo * OWN, hi * OWN)
        total = jnp.dot(mine[rows, :], w_here[...], preferred_element_type=F32)
        total += jnp.dot(theirs[rows, :], w_other[...], preferred_element_type=F32)
        for i in range(lo, hi):
            ref = (own, out1, out2, out3)[i]
            ref[...] = total[(i - lo) * OWN : (i - lo + 1) * OWN].astype(ref.dtype)


def output(mine, theirs, w_here, w_other):
    vmem = pl.BlockSpec(memory_space=pltpu.VMEM)
    return pl.pallas_call(
        output_kernel,
        out_shape=[jax.ShapeDtypeStruct((OWN, D), F32)]
        + [jax.ShapeDtypeStruct((OWN, D), BF16)] * 3,
        in_specs=[vmem] * 4,
        out_specs=[vmem] * 4,
        compiler_params=pltpu.CompilerParams(vmem_limit_bytes=VMEM_LIMIT),
        name="output",
    )(mine, theirs, w_here, w_other)


def select_gate(modulation, second, text):
    video_cols = modulation[:, 2 * D : 3 * D]
    text_cols = modulation[:, 5 * D : 6 * D]
    video_pick = jnp.where(second, video_cols[1][None, :], video_cols[0][None, :])
    text_pick = jnp.where(second, text_cols[1][None, :], text_cols[0][None, :])
    return jnp.where(text, text_pick, video_pick)


def local(
    tokens, w_query, w_key, w_value, w_out, w_mod, gain_query, gain_key, timesteps,
    video_lengths, piece_table,
):
    x, core = lax.axis_index("x"), lax.axis_index("core")
    z = lax.axis_index("z")
    y = lax.axis_index("yhi") * 2 + lax.axis_index("ylo")
    boundary = TEXT + video_lengths[0]

    across = [tokens] + [shift_x(tokens, step) for step in SHIFTS]
    chunks = across + [swap_core(chunk) for chunk in across]

    w_other = swap_core(w_out)

    act = jax.nn.silu(time_features(timesteps)).astype(BF16)
    part_mod = jnp.dot(act, w_mod, preferred_element_type=F32)
    width = part_mod.shape[1]
    packed = jnp.pad(part_mod.reshape(2 * width), (0, 384 - 2 * width)).reshape(3, 128)
    tiles_axes = ("ylo", "z", "yhi")
    spread = lax.all_to_all(
        jnp.broadcast_to(packed[None], (16, 3, 128)), tiles_axes, 0, 0, tiled=True
    )
    spread = lax.all_to_all(
        jnp.broadcast_to(spread[None], (8, 16, 3, 128)), ("x", "core"), 0, 0, tiled=True
    )
    spread = spread.transpose(1, 0, 2, 3).reshape(128, 384)
    modulation = jnp.stack(
        [spread[:, :width].reshape(128 * width), spread[:, width : 2 * width].reshape(128 * width)]
    )

    back = jnp.array([0, 1, -1, 2], jnp.int32)
    z_ring = (z - back) % 4
    y_ring = (y - back) % 4
    z_tiles = ((y % 2) * 4 + z_ring) * 2 + y // 2
    y_tiles = ((y_ring % 2) * 4 + z) * 2 + y_ring // 2
    tiles = jnp.concatenate([z_tiles, y_tiles])
    pieces = jnp.sum(
        jnp.where(
            tiles[:, None] == jnp.arange(16, dtype=jnp.int32)[None, :], piece_table[None, :], 0
        ),
        axis=1,
    )
    limits_a = jnp.clip(boundary - pieces * CAP, 0, CAP)
    limits_b = jnp.concatenate([limits_a[4:], limits_a[:4]])
    piece = pieces[0]
    x_ring = (x - back) % 4
    starts = jnp.concatenate([(x_ring * 2 + core) * OWN, (x_ring * 2 + 1 - core) * OWN])
    info = jnp.concatenate([starts, jnp.stack([piece, boundary])])

    cos, sin = rope_tables(piece, boundary)
    along_z, along_y = project(
        info, chunks, modulation, w_query, w_key, w_value, cos, sin, gain_query[None, :],
        gain_key[None, :],
    )
    from_z = [along_z] + [shift_z(along_z, step) for step in SHIFTS]
    from_y = [along_y] + [shift_y(along_y, step) for step in SHIFTS]
    near_a = attend(limits_a, from_z[:3], from_y[:3], (0, 1, 2), "near_a")[0]
    own_a, *parts_a = attend(limits_a, from_z, from_y, (0, 1, 2, 3), "far_a", near_a)
    sent_a = [shift_z(part, -step) for part, step in zip(parts_a, SHIFTS)]
    limits_b, _ = lax.optimization_barrier((limits_b, parts_a[0]))
    parts_b = attend(limits_b, from_y[1:], from_z, (1, 2, 3), "rest_b")
    sent_b = [shift_y(part, -step) for part, step in zip(parts_b, SHIFTS)]
    limits_b, _ = lax.optimization_barrier((limits_b, (parts_b[0], sent_a)))
    own_b = attend(limits_b, from_y[:1], from_z, (0,), "own_b")[0]

    ahead = (x + back) % 4
    order = jnp.concatenate([(ahead * 2 + 1 - core) * OWN, (ahead * 2 + core) * OWN])
    theirs, mine = merge(order, own_a, sent_a, own_b, sent_b)
    received = swap_core(theirs)
    sums = output(mine, received, w_out, w_other)
    projection = sums[0]
    for share, step in zip(sums[1:], SHIFTS):
        projection = projection + shift_x(share, step).astype(F32)

    own_token = piece * CAP + starts[0] + jnp.arange(OWN, dtype=jnp.int32)[:, None]
    second = own_token >= boundary
    text = own_token - jnp.where(second, boundary, 0) < TEXT
    gate = select_gate(modulation, second, text)
    return (gate * projection).astype(BF16)


def solution(mesh):
    fine = Mesh(mesh.devices.reshape(2, 4, 2, 4, 2), AXES)
    tensor = ("x", "core")
    placed = (
        P(AXES, None),
        P(None, tensor),
        P(None, tensor),
        P(None, tensor),
        P(tensor, None),
        P(None, AXES),
        P(),
        P(),
        P(),
        P(),
        P(),
    )
    return jax.shard_map(
        local, mesh=fine, in_specs=placed, out_specs=P(AXES, None), check_vma=False
    )
```

```python
import functools
import math

import jax
import jax.numpy as jnp
from jax import lax
from jax.experimental import pallas as pl
from jax.experimental.pallas import tpu as pltpu
from jax.sharding import Mesh, PartitionSpec as P

HD = 64
TE = 512
TEXT = 226
HP = 30
WP = 45
CAP = 640
D = 3072
BLK = 128
OWN = 80
BIG = 16384.0
F32 = jnp.float32
BF16 = jnp.bfloat16

AXES = ("ylo", "z", "yhi", "x", "core")
Y_AXES = ("ylo", "yhi")
Y_INDEX = (0, 2, 1, 3)
VMEM_LIMIT = 60 * 1024 * 1024
SHIFTS = (1, -1, 2)


def shift_x(value, step):
    return lax.ppermute(value, "x", [(i, (i + step) % 4) for i in range(4)])


def shift_z(value, step):
    return lax.ppermute(value, "z", [(i, (i + step) % 4) for i in range(4)])


def shift_y(value, step):
    return lax.ppermute(value, Y_AXES, [(Y_INDEX[i], Y_INDEX[(i + step) % 4]) for i in range(4)])


def swap_core(value):
    return lax.ppermute(value, "core", [(0, 1), (1, 0)])


def time_features(timesteps):
    half_dim = TE // 2
    freqs = jnp.exp(-math.log(10000.0) * jnp.arange(half_dim, dtype=F32) / half_dim)
    angles = timesteps.astype(F32)[:, None] * freqs[None, :]
    return jnp.concatenate([jnp.cos(angles), jnp.sin(angles)], axis=1)


def rope_tables(piece, boundary):
    token = piece * CAP + lax.broadcasted_iota(jnp.int32, (CAP, 2 * HD), 0)
    lane = lax.broadcasted_iota(jnp.int32, (CAP, 2 * HD), 1)
    inner = token - jnp.where(token >= boundary, boundary, 0)
    is_text = inner < TEXT
    video = jnp.maximum(inner - TEXT, 0)
    frame = video // (HP * WP)
    height = video // WP % HP
    width = video % WP
    pair = lane % HD // 2
    time_pairs = HD // 8
    space_pairs = 3 * HD // 16
    freq_time = 10000.0 ** (-jnp.arange(0, HD // 4, 2, dtype=F32) / (HD // 4))
    freq_space = 10000.0 ** (-jnp.arange(0, 3 * HD // 8, 2, dtype=F32) / (3 * HD // 8))
    freq = jnp.concatenate([freq_time, freq_space, freq_space])
    freq = jnp.tile(jnp.repeat(freq, 2), 2)[None, :]
    place = jnp.where(
        pair < time_pairs, frame, jnp.where(pair < time_pairs + space_pairs, height, width)
    )
    angle = place.astype(F32) * freq
    cosine = jnp.where(is_text, 1.0, jnp.cos(angle))
    sine = jnp.where(is_text, 0.0, jnp.sin(angle))
    return cosine, jnp.where(lane % 2 == 0, -sine, sine)


def project_kernel(
    info, c0, c1, c2, c3, c4, c5, c6, c7, mods, wq_far, wk_far, wv_far, cos, sin, gq, gk,
    along_z, along_y, rows_in, wq, wk, wv, qa, kva, qb, kvb, middle, sems,
):
    chunks = (c0, c1, c2, c3, c4, c5, c6, c7)
    arrivals = [
        pltpu.make_async_copy(
            chunk, rows_in.at[pl.ds(pl.multiple_of(info[i], 16), OWN), :], sems.at[3 + i]
        )
        for i, chunk in enumerate(chunks)
    ]
    copies = [
        pltpu.make_async_copy(source, target, sems.at[i])
        for i, (source, target) in enumerate(((wq_far, wq), (wk_far, wk), (wv_far, wv)))
    ]
    for copy in arrivals + copies:
        copy.start()
    gain_q = jnp.concatenate([gq[...], gq[...]], axis=1)
    gain_k = jnp.concatenate([gk[...], gk[...]], axis=1)
    for copy in arrivals:
        copy.wait()
    piece = info[8]
    boundary = info[9]
    line = lax.broadcasted_iota(jnp.int32, (256, 128), 0)
    average = jnp.where(
        line % 128 // HD == lax.broadcasted_iota(jnp.int32, (256, 128), 1) // HD, 1.0 / HD, 0.0
    ).astype(BF16)
    even = lax.broadcasted_iota(jnp.int32, (BLK, 128), 1) % 2 == 0

    def head_mean(entries):
        high = entries.astype(BF16)
        low = (entries - high.astype(F32)).astype(BF16)
        return jnp.dot(
            jnp.concatenate([high, low], axis=1), average, preferred_element_type=F32
        )

    def head_prepare(entries, gain, block):
        center = entries - head_mean(entries)
        variance = head_mean(center * center)
        normed = center * lax.rsqrt(variance + 1e-06) * gain
        other = jnp.where(even, pltpu.roll(normed, 127, 1), pltpu.roll(normed, 1, 1))
        place = slice(block * BLK, (block + 1) * BLK)
        return normed * cos[place, :] + other * sin[place, :]

    for block in range(CAP // BLK):
        place = slice(block * BLK, (block + 1) * BLK)
        values = rows_in[place, :].astype(F32)
        center = values - jnp.mean(values, axis=1, keepdims=True)
        variance = jnp.mean(center * center, axis=1, keepdims=True)
        normed = center * lax.rsqrt(variance + 1e-05)
        token = piece * CAP + block * BLK + lax.broadcasted_iota(jnp.int32, (BLK, 1), 0)
        second = token >= boundary
        text = token - jnp.where(second, boundary, 0) < TEXT

        def pick(part):
            video_cols = slice(part * D, (part + 1) * D)
            text_cols = slice((part + 3) * D, (part + 4) * D)
            video_pick = jnp.where(second, mods[1:2, video_cols], mods[0:1, video_cols])
            text_pick = jnp.where(second, mods[1:2, text_cols], mods[0:1, text_cols])
            return jnp.where(text, text_pick, video_pick)

        modded = (normed * (1.0 + pick(1)) + pick(0)).astype(BF16)
        if block == 0:
            for copy in copies:
                copy.wait()
        query = jnp.dot(modded, wq[...], preferred_element_type=F32)
        key = jnp.dot(modded, wk[...], preferred_element_type=F32)
        value = jnp.dot(modded, wv[...], preferred_element_type=F32)
        base = block * 192
        for group in range(3):
            cols = slice(group * 128, (group + 1) * 128)
            q_turn = head_prepare(query[:, cols], gain_q, block).T.astype(BF16)
            v_turn = value[:, cols].T.astype(BF16)
            k_rows = head_prepare(key[:, cols], gain_k, block)
            if group == 0:
                qa[base : base + 128, :] = q_turn
                kva[960 + base : 960 + base + 128, :] = v_turn
                kva[place, :] = k_rows.astype(BF16)
            elif group == 1:
                qa[base + 128 : base + 192, :] = q_turn[:64]
                qb[base + 128 : base + 192, :] = q_turn[64:]
                kva[960 + base + 128 : 960 + base + 192, :] = v_turn[:64]
                kvb[960 + base + 128 : 960 + base + 192, :] = v_turn[64:]
                middle[place, :] = k_rows
            else:
                qb[base : base + 128, :] = q_turn
                kvb[960 + base : 960 + base + 128, :] = v_turn
                kvb[place, :] = k_rows.astype(BF16)
    left = lax.broadcasted_iota(jnp.int32, (CAP // 2, 128), 1) < HD
    upper = middle[: CAP // 2, :]
    lower = middle[CAP // 2 :, :]
    kva[CAP:960, :] = jnp.where(left, upper, pltpu.roll(lower, HD, 1)).astype(BF16)
    kvb[CAP:960, :] = jnp.where(left, pltpu.roll(upper, HD, 1), lower).astype(BF16)
    along_z[:960, :] = qa[...]
    along_z[960:, :] = kvb[...]
    along_y[:960, :] = qb[...]
    along_y[960:, :] = kva[...]


def project(info, chunks, mods, wq, wk, wv, cos, sin, gq, gk):
    vmem = pl.BlockSpec(memory_space=pltpu.VMEM)
    return pl.pallas_call(
        project_kernel,
        out_shape=[jax.ShapeDtypeStruct((2880, 128), BF16)] * 2,
        in_specs=[pl.BlockSpec(memory_space=pltpu.SMEM)]
        + [pl.BlockSpec(memory_space=pl.ANY)] * 8
        + [vmem]
        + [pl.BlockSpec(memory_space=pl.ANY)] * 3
        + [vmem] * 4,
        out_specs=[vmem] * 2,
        scratch_shapes=[pltpu.VMEM((CAP, D), BF16)]
        + [pltpu.VMEM((D, 384), BF16)] * 3
        + [pltpu.VMEM((960, 128), BF16), pltpu.VMEM((1920, 128), BF16)] * 2
        + [pltpu.VMEM((CAP, 128), F32), pltpu.SemaphoreType.DMA((11,))],
        compiler_params=pltpu.CompilerParams(vmem_limit_bytes=VMEM_LIMIT),
        name="project",
    )(info, *chunks, mods, wq, wk, wv, cos, sin, gq, gk)


def attend_kernel(limits, *refs, places, n_k, carried, last):
    n_q = len(places)
    queries, refs = refs[:n_q], refs[n_q:]
    keys, refs = refs[:n_k], refs[n_k:]
    if carried:
        before, refs = refs[0], refs[1:]
    n_out = n_q if last else 1
    outs, refs = refs[:n_out], refs[n_out:]
    qs, ks, vs, todo = refs[:4]
    acc = refs[4] if last else outs[0]
    scale = math.log2(math.e) / math.sqrt(HD)
    half = CAP // 2
    ones = jnp.where(lax.broadcasted_iota(jnp.int32, (16, CAP), 0) == 0, 1.0, 0.0).astype(BF16)
    blank = jnp.zeros((HD, CAP), BF16)

    kinds = [
        jnp.where(limits[4 + tile] == CAP, 0, jnp.where(limits[4 + tile] == 0, 2, 1))
        for tile in range(n_k)
    ]
    slots = []
    only_first = jnp.int32(0)
    only_second = jnp.int32(0)
    key_limit = jnp.int32(0)
    for tile in range(n_k):
        slot = jnp.int32(0)
        for other in range(n_k):
            if other < tile:
                slot = slot + jnp.where(kinds[other] <= kinds[tile], 1, 0)
            elif other > tile:
                slot = slot + jnp.where(kinds[other] < kinds[tile], 1, 0)
        slots.append(slot)
        only_first = only_first + jnp.where(kinds[tile] == 0, 1, 0)
        only_second = only_second + jnp.where(kinds[tile] == 2, 1, 0)
        key_limit = key_limit + limits[4 + tile]
    for i, place in enumerate(places):
        has_first = limits[place] > 0
        has_second = limits[place] < CAP
        todo[16 + i] = limits[place]
        if carried and place != 3:
            shared = (has_first & (limits[7] > 0)) | (has_second & (limits[7] < CAP))
            todo[i] = slots[3]
            todo[8 + i] = jnp.where(shared, 1, 0)
        else:
            low = jnp.where(has_first, 0, only_first)
            todo[i] = low
            todo[8 + i] = jnp.where(has_second, n_k, n_k - only_second) - low

    for tile in range(n_k):
        start = pl.multiple_of(slots[tile] * CAP, 64)
        ks[0, pl.ds(start, CAP), :] = keys[tile][:CAP, :]
        end = keys[tile][CAP:960, :]
        ks[1, pl.ds(start, half), :] = end
        ks[1, pl.ds(start + half, half), :] = jnp.concatenate([end[:, HD:], end[:, :HD]], axis=1)
        vs[pl.ds(pl.multiple_of(slots[tile] * 960, 64), 960), :] = keys[tile][960:, :]
    for i, place in enumerate(places):
        for head in range(3):
            at = HD if head == 1 else 0
            qs[i, head, HD - at : 2 * HD - at, :] = blank
            for block in range(5):
                row = 192 * block + HD * head
                cols = slice(128 * block, 128 * block + 128)
                qs[i, head, at : at + HD, cols] = queries[i][row : row + HD, :]
        if carried and place != 3:
            acc[i] = before[i]
        else:
            acc[i] = jnp.zeros((3, 80, CAP), F32)

    def part(i, head, slot, count, masked):
        first = pl.multiple_of(slot * CAP, 64)
        bank = jnp.where(head == 2, 1, 0)
        scores = jnp.dot(
            ks[bank, pl.ds(first, count * CAP), :], qs[i, head], preferred_element_type=F32
        )
        weights = jnp.exp2(scores * scale).astype(BF16)
        columns = []
        for block in range(5 * count):
            start = slot * 960 + head * HD + 192 * block
            columns.append(vs[pl.ds(pl.multiple_of(start, HD), HD), :])
        value = jnp.concatenate(
            [jnp.concatenate(columns, axis=1), jnp.concatenate([ones] * count, axis=1)], axis=0
        )
        place = first + lax.broadcasted_iota(jnp.int32, value.shape, 1)
        k_second = jnp.where(place >= key_limit, 1, 0)
        nothing = jnp.zeros_like(value)
        if masked:
            value = jnp.concatenate(
                [
                    jnp.where(k_second == 0, value, nothing),
                    jnp.where(k_second == 1, value, nothing),
                ],
                axis=0,
            )
            both = jnp.dot(value, weights, preferred_element_type=F32)
            q_second = lax.broadcasted_iota(jnp.int32, (80, CAP), 1) >= todo[16 + i]
            acc[i, head] += jnp.where(q_second, both[80:], both[:80])
        else:
            sample = jnp.where(todo[16 + i] > 0, 0, 1)
            value = jnp.where(k_second == sample, value, nothing)
            acc[i, head] += jnp.dot(value, weights, preferred_element_type=F32)

    def heads(i, slot, count, masked):
        def one_head(head, rest):
            part(i, head, slot, count, masked)
            return rest

        lax.fori_loop(0, 3, one_head, 0)

    def q_tile(i, carry):
        low = todo[i]
        count = todo[8 + i]
        limit = todo[16 + i]
        mixed = (limit > 0) & (limit < CAP)

        @pl.when(mixed)
        def _():
            def one(step, inner):
                heads(i, low + step, 1, True)
                return inner

            lax.fori_loop(0, count, one, 0)

        @pl.when(jnp.logical_not(mixed))
        def _():
            def two(step, inner):
                heads(i, low + 2 * step, 2, False)
                return inner

            lax.fori_loop(0, count // 2, two, 0)

            @pl.when(count % 2 == 1)
            def _():
                heads(i, low + count - 1, 1, False)

        return carry

    lax.fori_loop(0, n_q, q_tile, 0)
    if last:
        for i, (place, ref) in enumerate(zip(places, outs)):
            if place == 0:
                ref[...] = acc[i]
                continue
            sums = jnp.concatenate([acc[i, head, HD : HD + 1, :] for head in range(3)], axis=0)
            high = sums.astype(BF16)
            low = (sums - high.astype(F32)).astype(BF16)
            for head in range(3):
                ref[HD * head : HD * head + HD, :] = acc[i, head, :HD, :].astype(BF16)
            ref[192:195, :] = high
            ref[195:198, :] = low
            ref[198:208, :] = jnp.zeros((10, CAP), BF16)


def attend(limits, queries, keys, places, name, before=None):
    vmem = pl.BlockSpec(memory_space=pltpu.VMEM)
    n_q, n_k = len(places), len(keys)
    carried = before is not None
    last = n_k == 4
    if last:
        out_shape = [
            jax.ShapeDtypeStruct((208, CAP), BF16)
            if place
            else jax.ShapeDtypeStruct((3, 80, CAP), F32)
            for place in places
        ]
    else:
        out_shape = [jax.ShapeDtypeStruct((n_q, 3, 80, CAP), F32)]
    scratch = [
        pltpu.VMEM((n_q, 3, 128, CAP), BF16),
        pltpu.VMEM((2, n_k * CAP, 128), BF16),
        pltpu.VMEM((n_k * 960, 128), BF16),
        pltpu.SMEM((24,), jnp.int32),
    ]
    if last:
        scratch.append(pltpu.VMEM((n_q, 3, 80, CAP), F32))
    q_spec = pl.BlockSpec((960, 128), lambda i: (0, 0))
    k_spec = pl.BlockSpec((pl.Element(1920), pl.Element(128)), lambda i: (960, 0))
    operands = [limits, *queries, *keys] + ([before] if carried else [])
    specs = [pl.BlockSpec(memory_space=pltpu.SMEM)] + [q_spec] * n_q + [k_spec] * n_k
    return pl.pallas_call(
        functools.partial(attend_kernel, places=places, n_k=n_k, carried=carried, last=last),
        out_shape=out_shape,
        grid=(1,),
        in_specs=specs + [vmem] * (len(operands) - len(specs)),
        out_specs=[vmem] * len(out_shape),
        scratch_shapes=scratch,
        cost_estimate=pl.CostEstimate(flops=1000, transcendentals=0, bytes_accessed=1000),
        compiler_params=pltpu.CompilerParams(vmem_limit_bytes=VMEM_LIMIT),
        name=name,
    )(*operands)


def merge_kernel(
    order, own_a, a1, a2, a3, own_b, b1, b2, b3, theirs, mine, turned, rows
):
    for own, others, heads in (
        (own_a, (a1, a2, a3), (0, 1, 2)),
        (own_b, (b1, b2, b3), (4, 5, 3)),
    ):
        for place, head in enumerate(heads):
            total = own[place, :HD, :]
            share = own[place, HD : HD + 1, :]
            for ref in others:
                total = total + ref[HD * place : HD * place + HD, :].astype(F32)
                tail = ref[192:208, :].astype(F32)
                share = share + tail[place : place + 1, :] + tail[3 + place : 4 + place, :]
            turned[HD * head : HD * head + HD, :] = total / share

    def turn(block, carry):
        place = pl.ds(pl.multiple_of(block * 128, 128), 128)
        for group in range(3):
            cols = slice(group * 128, group * 128 + 128)
            rows[place, cols] = turned[cols, place].T.astype(BF16)
        return carry

    lax.fori_loop(0, 5, turn, 0)
    for i in range(4):
        start = pl.multiple_of(order[i], 16)
        theirs[i * OWN : (i + 1) * OWN, :] = rows[pl.ds(start, OWN), :]
        start = pl.multiple_of(order[4 + i], 16)
        mine[i * OWN : (i + 1) * OWN, :] = rows[pl.ds(start, OWN), :]


def merge(order, own_a, others_a, own_b, others_b):
    vmem = pl.BlockSpec(memory_space=pltpu.VMEM)
    return pl.pallas_call(
        merge_kernel,
        out_shape=[jax.ShapeDtypeStruct((4 * OWN, 384), BF16)] * 2,
        in_specs=[pl.BlockSpec(memory_space=pltpu.SMEM)] + [vmem] * 8,
        out_specs=[vmem] * 2,
        scratch_shapes=[pltpu.VMEM((384, CAP), F32), pltpu.VMEM((CAP, 384), BF16)],
        compiler_params=pltpu.CompilerParams(vmem_limit_bytes=VMEM_LIMIT),
        name="merge",
    )(order, own_a, *others_a, own_b, *others_b)


def far_output_kernel(mine, theirs, w_here, w_other, out):
    rows = slice(3 * OWN, 4 * OWN)

    def step(i, carry):
        cols = pl.ds(pl.multiple_of(i * 768, 128), 768)
        total = jnp.dot(mine[rows, :], w_here[:, cols], preferred_element_type=F32)
        total += jnp.dot(theirs[rows, :], w_other[:, cols], preferred_element_type=F32)
        out[:, cols] = total.astype(BF16)
        return carry

    lax.fori_loop(0, D // 768, step, 0)


def far_output(mine, theirs, w_here, w_other):
    vmem = pl.BlockSpec(memory_space=pltpu.VMEM)
    return pl.pallas_call(
        far_output_kernel,
        out_shape=jax.ShapeDtypeStruct((OWN, D), BF16),
        in_specs=[vmem] * 4,
        out_specs=vmem,
        cost_estimate=pl.CostEstimate(flops=1000, transcendentals=0, bytes_accessed=1000),
        compiler_params=pltpu.CompilerParams(vmem_limit_bytes=VMEM_LIMIT),
        name="far_output",
    )(mine, theirs, w_here, w_other)


def near_output_kernel(mine, theirs, r1, r2, *refs):
    far, out, held, left, sems = refs[:6], refs[6], refs[7], refs[8], refs[9]
    for i, source in enumerate(far):
        pltpu.make_async_copy(source, held.at[i], sems.at[i]).start()
    rows = (mine[:OWN, :], theirs[:OWN, :], r1[:OWN, :], r1[OWN:, :], r2[:OWN, :], r2[OWN:, :])
    for i, entries in enumerate(rows):
        left[i] = entries
    out[...] = jnp.zeros_like(out)

    def step(i, carry):
        pltpu.make_async_copy(far[0], held.at[i], sems.at[i]).wait()
        out[...] += jnp.dot(left[i], held[i], preferred_element_type=F32)
        return carry

    lax.fori_loop(0, 6, step, 0)


def near_output(mine, theirs, r1, r2, weights):
    vmem = pl.BlockSpec(memory_space=pltpu.VMEM)
    return pl.pallas_call(
        near_output_kernel,
        out_shape=jax.ShapeDtypeStruct((OWN, D), F32),
        in_specs=[vmem] * 4 + [pl.BlockSpec(memory_space=pl.ANY)] * 6,
        out_specs=vmem,
        scratch_shapes=[
            pltpu.VMEM((6, 384, D), BF16),
            pltpu.VMEM((6, OWN, 384), BF16),
            pltpu.SemaphoreType.DMA((6,)),
        ],
        compiler_params=pltpu.CompilerParams(vmem_limit_bytes=VMEM_LIMIT),
        name="near_output",
    )(mine, theirs, r1, r2, *weights)


def select_gate(modulation, second, text):
    video_cols = modulation[:, 2 * D : 3 * D]
    text_cols = modulation[:, 5 * D : 6 * D]
    video_pick = jnp.where(second, video_cols[1][None, :], video_cols[0][None, :])
    text_pick = jnp.where(second, text_cols[1][None, :], text_cols[0][None, :])
    return jnp.where(text, text_pick, video_pick)


def local(
    tokens, w_query, w_key, w_value, w_out, w_mod, gain_query, gain_key, timesteps,
    video_lengths, piece_table,
):
    x, core = lax.axis_index("x"), lax.axis_index("core")
    z = lax.axis_index("z")
    y = lax.axis_index("yhi") * 2 + lax.axis_index("ylo")
    boundary = TEXT + video_lengths[0]

    across = [tokens] + [shift_x(tokens, step) for step in SHIFTS]
    chunks = across + [swap_core(chunk) for chunk in across]

    w_other = swap_core(w_out)

    act = jax.nn.silu(time_features(timesteps)).astype(BF16)
    part_mod = jnp.dot(act, w_mod, preferred_element_type=F32)
    width = part_mod.shape[1]
    packed = jnp.pad(part_mod.reshape(2 * width), (0, 384 - 2 * width)).reshape(3, 128)
    tiles_axes = ("ylo", "z", "yhi")
    spread = lax.all_to_all(
        jnp.broadcast_to(packed[None], (16, 3, 128)), tiles_axes, 0, 0, tiled=True
    )
    spread = lax.all_to_all(
        jnp.broadcast_to(spread[None], (8, 16, 3, 128)), ("x", "core"), 0, 0, tiled=True
    )
    spread = spread.transpose(1, 0, 2, 3).reshape(128, 384)
    modulation = jnp.stack(
        [spread[:, :width].reshape(128 * width), spread[:, width : 2 * width].reshape(128 * width)]
    )

    back = jnp.array([0, 1, -1, 2], jnp.int32)
    z_ring = (z - back) % 4
    y_ring = (y - back) % 4
    z_tiles = ((y % 2) * 4 + z_ring) * 2 + y // 2
    y_tiles = ((y_ring % 2) * 4 + z) * 2 + y_ring // 2
    tiles = jnp.concatenate([z_tiles, y_tiles])
    pieces = jnp.sum(
        jnp.where(
            tiles[:, None] == jnp.arange(16, dtype=jnp.int32)[None, :], piece_table[None, :], 0
        ),
        axis=1,
    )
    limits_a = jnp.clip(boundary - pieces * CAP, 0, CAP)
    limits_b = jnp.concatenate([limits_a[4:], limits_a[:4]])
    piece = pieces[0]
    x_ring = (x - back) % 4
    starts = jnp.concatenate([(x_ring * 2 + core) * OWN, (x_ring * 2 + 1 - core) * OWN])
    info = jnp.concatenate([starts, jnp.stack([piece, boundary])])

    cos, sin = rope_tables(piece, boundary)
    along_z, along_y = project(
        info, chunks, modulation, w_query, w_key, w_value, cos, sin, gain_query[None, :],
        gain_key[None, :],
    )
    from_z = [along_z] + [shift_z(along_z, step) for step in SHIFTS]
    from_y = [along_y] + [shift_y(along_y, step) for step in SHIFTS]
    limits_a, w_other, w_late, _ = lax.optimization_barrier(
        (limits_a, w_other, w_out, (from_z[1:3], from_y[1:3]))
    )
    w_behind, w_ahead = shift_x(w_late, 1), shift_x(w_late, -1)
    v_behind, v_ahead = swap_core(w_behind), swap_core(w_ahead)
    near_a = attend(limits_a, from_z[:3], from_y[:3], (0, 1, 2), "near_a")[0]
    own_a, *parts_a = attend(limits_a, from_z, from_y, (0, 1, 2, 3), "far_a", near_a)
    sent_a = [shift_z(part, -step) for part, step in zip(parts_a, SHIFTS)]
    limits_b, _ = lax.optimization_barrier((limits_b, parts_a[0]))
    parts_b = attend(limits_b, from_y[1:], from_z, (1, 2, 3), "rest_b")
    sent_b = [shift_y(part, -step) for part, step in zip(parts_b, SHIFTS)]
    limits_b, _ = lax.optimization_barrier((limits_b, (parts_b[0], sent_a)))
    own_b = attend(limits_b, from_y[:1], from_z, (0,), "own_b")[0]

    ahead = (x + back) % 4
    order = jnp.concatenate([(ahead * 2 + 1 - core) * OWN, (ahead * 2 + core) * OWN])
    theirs, mine = merge(order, own_a, sent_a, own_b, sent_b)
    received = swap_core(theirs)
    share = shift_x(far_output(mine, received, w_out, w_other), 2)
    arrived = []
    for i, step in ((1, 1), (2, -1)):
        rows = slice(i * OWN, (i + 1) * OWN)
        arrived.append(shift_x(jnp.concatenate([mine[rows], received[rows]]), step))
    projection = near_output(
        mine, received, *arrived, (w_out, w_other, w_behind, v_behind, w_ahead, v_ahead)
    )
    projection = projection + share.astype(F32)

    own_token = piece * CAP + starts[0] + jnp.arange(OWN, dtype=jnp.int32)[:, None]
    second = own_token >= boundary
    text = own_token - jnp.where(second, boundary, 0) < TEXT
    gate = select_gate(modulation, second, text)
    return (gate * projection).astype(BF16)


def solution(mesh):
    fine = Mesh(mesh.devices.reshape(2, 4, 2, 4, 2), AXES)
    tensor = ("x", "core")
    placed = (
        P(AXES, None),
        P(None, tensor),
        P(None, tensor),
        P(None, tensor),
        P(tensor, None),
        P(None, AXES),
        P(),
        P(),
        P(),
        P(),
        P(),
    )
    return jax.shard_map(
        local, mesh=fine, in_specs=placed, out_specs=P(AXES, None), check_vma=False
    )
```

```python
import functools
import math

import jax
import jax.numpy as jnp
from jax import lax
from jax.experimental import pallas as pl
from jax.experimental.pallas import tpu as pltpu
from jax.sharding import Mesh, PartitionSpec as P

HD = 64
TE = 512
TEXT = 226
HP = 30
WP = 45
CAP = 640
D = 3072
BLK = 128
OWN = 80
BIG = 16384.0
F32 = jnp.float32
BF16 = jnp.bfloat16

AXES = ("ylo", "z", "yhi", "x", "core")
Y_AXES = ("ylo", "yhi")
Y_INDEX = (0, 2, 1, 3)
VMEM_LIMIT = 60 * 1024 * 1024
SHIFTS = (1, -1, 2)


def shift_x(value, step):
    return lax.ppermute(value, "x", [(i, (i + step) % 4) for i in range(4)])


def shift_z(value, step):
    return lax.ppermute(value, "z", [(i, (i + step) % 4) for i in range(4)])


def shift_y(value, step):
    return lax.ppermute(value, Y_AXES, [(Y_INDEX[i], Y_INDEX[(i + step) % 4]) for i in range(4)])


def swap_core(value):
    return lax.ppermute(value, "core", [(0, 1), (1, 0)])


def time_features(timesteps):
    half_dim = TE // 2
    freqs = jnp.exp(-math.log(10000.0) * jnp.arange(half_dim, dtype=F32) / half_dim)
    angles = timesteps.astype(F32)[:, None] * freqs[None, :]
    return jnp.concatenate([jnp.cos(angles), jnp.sin(angles)], axis=1)


def rope_tables(piece, boundary):
    token = piece * CAP + lax.broadcasted_iota(jnp.int32, (CAP, 2 * HD), 0)
    lane = lax.broadcasted_iota(jnp.int32, (CAP, 2 * HD), 1)
    inner = token - jnp.where(token >= boundary, boundary, 0)
    is_text = inner < TEXT
    video = jnp.maximum(inner - TEXT, 0)
    frame = video // (HP * WP)
    height = video // WP % HP
    width = video % WP
    pair = lane % HD // 2
    time_pairs = HD // 8
    space_pairs = 3 * HD // 16
    freq_time = 10000.0 ** (-jnp.arange(0, HD // 4, 2, dtype=F32) / (HD // 4))
    freq_space = 10000.0 ** (-jnp.arange(0, 3 * HD // 8, 2, dtype=F32) / (3 * HD // 8))
    freq = jnp.concatenate([freq_time, freq_space, freq_space])
    freq = jnp.tile(jnp.repeat(freq, 2), 2)[None, :]
    place = jnp.where(
        pair < time_pairs, frame, jnp.where(pair < time_pairs + space_pairs, height, width)
    )
    angle = place.astype(F32) * freq
    cosine = jnp.where(is_text, 1.0, jnp.cos(angle))
    sine = jnp.where(is_text, 0.0, jnp.sin(angle))
    return cosine, jnp.where(lane % 2 == 0, -sine, sine)


def project_kernel(
    info, c0, c1, c2, c3, c4, c5, c6, c7, mods, wq_far, wk_far, wv_far, cos, sin, gq, gk,
    along_z, along_y, rows_in, wq, wk, wv, qa, kva, qb, kvb, middle, sems,
):
    chunks = (c0, c1, c2, c3, c4, c5, c6, c7)
    arrivals = [
        pltpu.make_async_copy(
            chunk, rows_in.at[pl.ds(pl.multiple_of(info[i], 16), OWN), :], sems.at[3 + i]
        )
        for i, chunk in enumerate(chunks)
    ]
    copies = [
        pltpu.make_async_copy(source, target, sems.at[i])
        for i, (source, target) in enumerate(((wq_far, wq), (wk_far, wk), (wv_far, wv)))
    ]
    for copy in arrivals + copies:
        copy.start()
    gain_q = jnp.concatenate([gq[...], gq[...]], axis=1)
    gain_k = jnp.concatenate([gk[...], gk[...]], axis=1)
    for copy in arrivals:
        copy.wait()
    piece = info[8]
    boundary = info[9]
    line = lax.broadcasted_iota(jnp.int32, (256, 128), 0)
    average = jnp.where(
        line % 128 // HD == lax.broadcasted_iota(jnp.int32, (256, 128), 1) // HD, 1.0 / HD, 0.0
    ).astype(BF16)
    even = lax.broadcasted_iota(jnp.int32, (BLK, 128), 1) % 2 == 0

    def head_mean(entries):
        high = entries.astype(BF16)
        low = (entries - high.astype(F32)).astype(BF16)
        return jnp.dot(
            jnp.concatenate([high, low], axis=1), average, preferred_element_type=F32
        )

    def head_prepare(entries, gain, block):
        center = entries - head_mean(entries)
        variance = head_mean(center * center)
        normed = center * lax.rsqrt(variance + 1e-06) * gain
        other = jnp.where(even, pltpu.roll(normed, 127, 1), pltpu.roll(normed, 1, 1))
        place = slice(block * BLK, (block + 1) * BLK)
        return normed * cos[place, :] + other * sin[place, :]

    for block in range(CAP // BLK):
        place = slice(block * BLK, (block + 1) * BLK)
        values = rows_in[place, :].astype(F32)
        center = values - jnp.mean(values, axis=1, keepdims=True)
        variance = jnp.mean(center * center, axis=1, keepdims=True)
        normed = center * lax.rsqrt(variance + 1e-05)
        token = piece * CAP + block * BLK + lax.broadcasted_iota(jnp.int32, (BLK, 1), 0)
        second = token >= boundary
        text = token - jnp.where(second, boundary, 0) < TEXT

        def pick(part):
            video_cols = slice(part * D, (part + 1) * D)
            text_cols = slice((part + 3) * D, (part + 4) * D)
            video_pick = jnp.where(second, mods[1:2, video_cols], mods[0:1, video_cols])
            text_pick = jnp.where(second, mods[1:2, text_cols], mods[0:1, text_cols])
            return jnp.where(text, text_pick, video_pick)

        modded = (normed * (1.0 + pick(1)) + pick(0)).astype(BF16)
        if block == 0:
            for copy in copies:
                copy.wait()
        query = jnp.dot(modded, wq[...], preferred_element_type=F32)
        key = jnp.dot(modded, wk[...], preferred_element_type=F32)
        value = jnp.dot(modded, wv[...], preferred_element_type=F32)
        base = block * 192
        for group in range(3):
            cols = slice(group * 128, (group + 1) * 128)
            q_turn = head_prepare(query[:, cols], gain_q, block).T.astype(BF16)
            v_turn = value[:, cols].T.astype(BF16)
            k_rows = head_prepare(key[:, cols], gain_k, block)
            if group == 0:
                qa[base : base + 128, :] = q_turn
                kva[960 + base : 960 + base + 128, :] = v_turn
                kva[place, :] = k_rows.astype(BF16)
            elif group == 1:
                qa[base + 128 : base + 192, :] = q_turn[:64]
                qb[base + 128 : base + 192, :] = q_turn[64:]
                kva[960 + base + 128 : 960 + base + 192, :] = v_turn[:64]
                kvb[960 + base + 128 : 960 + base + 192, :] = v_turn[64:]
                middle[place, :] = k_rows
            else:
                qb[base : base + 128, :] = q_turn
                kvb[960 + base : 960 + base + 128, :] = v_turn
                kvb[place, :] = k_rows.astype(BF16)
    left = lax.broadcasted_iota(jnp.int32, (CAP // 2, 128), 1) < HD
    upper = middle[: CAP // 2, :]
    lower = middle[CAP // 2 :, :]
    kva[CAP:960, :] = jnp.where(left, upper, pltpu.roll(lower, HD, 1)).astype(BF16)
    kvb[CAP:960, :] = jnp.where(left, pltpu.roll(upper, HD, 1), lower).astype(BF16)
    along_z[:960, :] = qa[...]
    along_z[960:, :] = kvb[...]
    along_y[:960, :] = qb[...]
    along_y[960:, :] = kva[...]


def project(info, chunks, mods, wq, wk, wv, cos, sin, gq, gk):
    vmem = pl.BlockSpec(memory_space=pltpu.VMEM)
    return pl.pallas_call(
        project_kernel,
        out_shape=[jax.ShapeDtypeStruct((2880, 128), BF16)] * 2,
        in_specs=[pl.BlockSpec(memory_space=pltpu.SMEM)]
        + [pl.BlockSpec(memory_space=pl.ANY)] * 8
        + [vmem]
        + [pl.BlockSpec(memory_space=pl.ANY)] * 3
        + [vmem] * 4,
        out_specs=[vmem] * 2,
        scratch_shapes=[pltpu.VMEM((CAP, D), BF16)]
        + [pltpu.VMEM((D, 384), BF16)] * 3
        + [pltpu.VMEM((960, 128), BF16), pltpu.VMEM((1920, 128), BF16)] * 2
        + [pltpu.VMEM((CAP, 128), F32), pltpu.SemaphoreType.DMA((11,))],
        compiler_params=pltpu.CompilerParams(vmem_limit_bytes=VMEM_LIMIT),
        name="project",
    )(info, *chunks, mods, wq, wk, wv, cos, sin, gq, gk)


def attend_kernel(limits, *refs, places, n_k, carried, last):
    n_q = len(places)
    queries, refs = refs[:n_q], refs[n_q:]
    keys, refs = refs[:n_k], refs[n_k:]
    if carried:
        before, refs = refs[0], refs[1:]
    n_out = n_q if last else 1
    outs, refs = refs[:n_out], refs[n_out:]
    qs, ks, vs, todo = refs[:4]
    acc = refs[4] if last else outs[0]
    scale = math.log2(math.e) / math.sqrt(HD)
    half = CAP // 2
    ones = jnp.where(lax.broadcasted_iota(jnp.int32, (16, CAP), 0) == 0, 1.0, 0.0).astype(BF16)
    blank = jnp.zeros((HD, CAP), BF16)

    kinds = [
        jnp.where(limits[4 + tile] == CAP, 0, jnp.where(limits[4 + tile] == 0, 2, 1))
        for tile in range(n_k)
    ]
    slots = []
    only_first = jnp.int32(0)
    only_second = jnp.int32(0)
    key_limit = jnp.int32(0)
    for tile in range(n_k):
        slot = jnp.int32(0)
        for other in range(n_k):
            if other < tile:
                slot = slot + jnp.where(kinds[other] <= kinds[tile], 1, 0)
            elif other > tile:
                slot = slot + jnp.where(kinds[other] < kinds[tile], 1, 0)
        slots.append(slot)
        only_first = only_first + jnp.where(kinds[tile] == 0, 1, 0)
        only_second = only_second + jnp.where(kinds[tile] == 2, 1, 0)
        key_limit = key_limit + limits[4 + tile]
    for i, place in enumerate(places):
        has_first = limits[place] > 0
        has_second = limits[place] < CAP
        todo[16 + i] = limits[place]
        if carried and place != 3:
            shared = (has_first & (limits[7] > 0)) | (has_second & (limits[7] < CAP))
            todo[i] = slots[3]
            todo[8 + i] = jnp.where(shared, 1, 0)
        else:
            low = jnp.where(has_first, 0, only_first)
            todo[i] = low
            todo[8 + i] = jnp.where(has_second, n_k, n_k - only_second) - low

    for tile in range(n_k):
        start = pl.multiple_of(slots[tile] * CAP, 64)
        ks[0, pl.ds(start, CAP), :] = keys[tile][:CAP, :]
        end = keys[tile][CAP:960, :]
        ks[1, pl.ds(start, half), :] = end
        ks[1, pl.ds(start + half, half), :] = jnp.concatenate([end[:, HD:], end[:, :HD]], axis=1)
        vs[pl.ds(pl.multiple_of(slots[tile] * 960, 64), 960), :] = keys[tile][960:, :]
    for i, place in enumerate(places):
        for head in range(3):
            at = HD if head == 1 else 0
            qs[i, head, HD - at : 2 * HD - at, :] = blank
            for block in range(5):
                row = 192 * block + HD * head
                cols = slice(128 * block, 128 * block + 128)
                qs[i, head, at : at + HD, cols] = queries[i][row : row + HD, :]
        if carried and place != 3:
            acc[i] = before[i]
        else:
            acc[i] = jnp.zeros((3, 80, CAP), F32)

    def part(i, head, slot, count, masked):
        first = pl.multiple_of(slot * CAP, 64)
        bank = jnp.where(head == 2, 1, 0)
        scores = jnp.dot(
            ks[bank, pl.ds(first, count * CAP), :], qs[i, head], preferred_element_type=F32
        )
        weights = jnp.exp2(scores * scale).astype(BF16)
        columns = []
        for block in range(5 * count):
            start = slot * 960 + head * HD + 192 * block
            columns.append(vs[pl.ds(pl.multiple_of(start, HD), HD), :])
        value = jnp.concatenate(
            [jnp.concatenate(columns, axis=1), jnp.concatenate([ones] * count, axis=1)], axis=0
        )
        place = first + lax.broadcasted_iota(jnp.int32, value.shape, 1)
        k_second = jnp.where(place >= key_limit, 1, 0)
        nothing = jnp.zeros_like(value)
        if masked:
            value = jnp.concatenate(
                [
                    jnp.where(k_second == 0, value, nothing),
                    jnp.where(k_second == 1, value, nothing),
                ],
                axis=0,
            )
            both = jnp.dot(value, weights, preferred_element_type=F32)
            q_second = lax.broadcasted_iota(jnp.int32, (80, CAP), 1) >= todo[16 + i]
            acc[i, head] += jnp.where(q_second, both[80:], both[:80])
        else:
            sample = jnp.where(todo[16 + i] > 0, 0, 1)
            value = jnp.where(k_second == sample, value, nothing)
            acc[i, head] += jnp.dot(value, weights, preferred_element_type=F32)

    def heads(i, slot, count, masked):
        def one_head(head, rest):
            part(i, head, slot, count, masked)
            return rest

        lax.fori_loop(0, 3, one_head, 0)

    def q_tile(i, carry):
        low = todo[i]
        count = todo[8 + i]
        limit = todo[16 + i]
        mixed = (limit > 0) & (limit < CAP)

        @pl.when(mixed)
        def _():
            def one(step, inner):
                heads(i, low + step, 1, True)
                return inner

            lax.fori_loop(0, count, one, 0)

        @pl.when(jnp.logical_not(mixed))
        def _():
            def two(step, inner):
                heads(i, low + 2 * step, 2, False)
                return inner

            lax.fori_loop(0, count // 2, two, 0)

            @pl.when(count % 2 == 1)
            def _():
                heads(i, low + count - 1, 1, False)

        return carry

    lax.fori_loop(0, n_q, q_tile, 0)
    if last:
        for i, (place, ref) in enumerate(zip(places, outs)):
            if place == 0:
                ref[...] = acc[i]
                continue
            sums = jnp.concatenate([acc[i, head, HD : HD + 1, :] for head in range(3)], axis=0)
            high = sums.astype(BF16)
            low = (sums - high.astype(F32)).astype(BF16)
            for head in range(3):
                ref[HD * head : HD * head + HD, :] = acc[i, head, :HD, :].astype(BF16)
            ref[192:195, :] = high
            ref[195:198, :] = low
            ref[198:208, :] = jnp.zeros((10, CAP), BF16)


def attend(limits, queries, keys, places, name, before=None):
    vmem = pl.BlockSpec(memory_space=pltpu.VMEM)
    n_q, n_k = len(places), len(keys)
    carried = before is not None
    last = n_k == 4
    if last:
        out_shape = [
            jax.ShapeDtypeStruct((208, CAP), BF16)
            if place
            else jax.ShapeDtypeStruct((3, 80, CAP), F32)
            for place in places
        ]
    else:
        out_shape = [jax.ShapeDtypeStruct((n_q, 3, 80, CAP), F32)]
    scratch = [
        pltpu.VMEM((n_q, 3, 128, CAP), BF16),
        pltpu.VMEM((2, n_k * CAP, 128), BF16),
        pltpu.VMEM((n_k * 960, 128), BF16),
        pltpu.SMEM((24,), jnp.int32),
    ]
    if last:
        scratch.append(pltpu.VMEM((n_q, 3, 80, CAP), F32))
    q_spec = pl.BlockSpec((960, 128), lambda i: (0, 0))
    k_spec = pl.BlockSpec((pl.Element(1920), pl.Element(128)), lambda i: (960, 0))
    operands = [limits, *queries, *keys] + ([before] if carried else [])
    specs = [pl.BlockSpec(memory_space=pltpu.SMEM)] + [q_spec] * n_q + [k_spec] * n_k
    return pl.pallas_call(
        functools.partial(attend_kernel, places=places, n_k=n_k, carried=carried, last=last),
        out_shape=out_shape,
        grid=(1,),
        in_specs=specs + [vmem] * (len(operands) - len(specs)),
        out_specs=[vmem] * len(out_shape),
        scratch_shapes=scratch,
        cost_estimate=pl.CostEstimate(flops=1000, transcendentals=0, bytes_accessed=1000),
        compiler_params=pltpu.CompilerParams(vmem_limit_bytes=VMEM_LIMIT),
        name=name,
    )(*operands)


def merge_kernel(
    order, own_a, a1, a2, a3, own_b, b1, b2, b3, theirs, mine, turned, rows
):
    for own, others, heads in (
        (own_a, (a1, a2, a3), (0, 1, 2)),
        (own_b, (b1, b2, b3), (4, 5, 3)),
    ):
        for place, head in enumerate(heads):
            total = own[place, :HD, :]
            share = own[place, HD : HD + 1, :]
            for ref in others:
                total = total + ref[HD * place : HD * place + HD, :].astype(F32)
                tail = ref[192:208, :].astype(F32)
                share = share + tail[place : place + 1, :] + tail[3 + place : 4 + place, :]
            turned[HD * head : HD * head + HD, :] = total / share

    def turn(block, carry):
        place = pl.ds(pl.multiple_of(block * 128, 128), 128)
        for group in range(3):
            cols = slice(group * 128, group * 128 + 128)
            rows[place, cols] = turned[cols, place].T.astype(BF16)
        return carry

    lax.fori_loop(0, 5, turn, 0)
    for i in range(4):
        start = pl.multiple_of(order[i], 16)
        theirs[i * OWN : (i + 1) * OWN, :] = rows[pl.ds(start, OWN), :]
        start = pl.multiple_of(order[4 + i], 16)
        mine[i * OWN : (i + 1) * OWN, :] = rows[pl.ds(start, OWN), :]


def merge(order, own_a, others_a, own_b, others_b):
    vmem = pl.BlockSpec(memory_space=pltpu.VMEM)
    return pl.pallas_call(
        merge_kernel,
        out_shape=[jax.ShapeDtypeStruct((4 * OWN, 384), BF16)] * 2,
        in_specs=[pl.BlockSpec(memory_space=pltpu.SMEM)] + [vmem] * 8,
        out_specs=[vmem] * 2,
        scratch_shapes=[pltpu.VMEM((384, CAP), F32), pltpu.VMEM((CAP, 384), BF16)],
        compiler_params=pltpu.CompilerParams(vmem_limit_bytes=VMEM_LIMIT),
        name="merge",
    )(order, own_a, *others_a, own_b, *others_b)


def far_output_kernel(mine, theirs, w_here, w_other, out):
    rows = slice(3 * OWN, 4 * OWN)

    def step(i, carry):
        cols = pl.ds(pl.multiple_of(i * 768, 128), 768)
        total = jnp.dot(mine[rows, :], w_here[:, cols], preferred_element_type=F32)
        total += jnp.dot(theirs[rows, :], w_other[:, cols], preferred_element_type=F32)
        out[:, cols] = total.astype(BF16)
        return carry

    lax.fori_loop(0, D // 768, step, 0)


def far_output(mine, theirs, w_here, w_other):
    vmem = pl.BlockSpec(memory_space=pltpu.VMEM)
    return pl.pallas_call(
        far_output_kernel,
        out_shape=jax.ShapeDtypeStruct((OWN, D), BF16),
        in_specs=[vmem] * 4,
        out_specs=vmem,
        cost_estimate=pl.CostEstimate(flops=1000, transcendentals=0, bytes_accessed=1000),
        compiler_params=pltpu.CompilerParams(vmem_limit_bytes=VMEM_LIMIT),
        name="far_output",
    )(mine, theirs, w_here, w_other)


def near_output_kernel(mine, theirs, r1, r2, *refs):
    far, out, held, left, sems = refs[:6], refs[6], refs[7], refs[8], refs[9]
    for i, source in enumerate(far):
        pltpu.make_async_copy(source, held.at[i], sems.at[i]).start()
    rows = (mine[:OWN, :], theirs[:OWN, :], r1[:OWN, :], r1[OWN:, :], r2[:OWN, :], r2[OWN:, :])
    for i, entries in enumerate(rows):
        left[i] = entries
    out[...] = jnp.zeros_like(out)

    def step(i, carry):
        pltpu.make_async_copy(far[0], held.at[i], sems.at[i]).wait()
        out[...] += jnp.dot(left[i], held[i], preferred_element_type=F32)
        return carry

    lax.fori_loop(0, 6, step, 0)


def near_output(mine, theirs, r1, r2, weights):
    vmem = pl.BlockSpec(memory_space=pltpu.VMEM)
    return pl.pallas_call(
        near_output_kernel,
        out_shape=jax.ShapeDtypeStruct((OWN, D), F32),
        in_specs=[vmem] * 4 + [pl.BlockSpec(memory_space=pl.ANY)] * 6,
        out_specs=vmem,
        scratch_shapes=[
            pltpu.VMEM((6, 384, D), BF16),
            pltpu.VMEM((6, OWN, 384), BF16),
            pltpu.SemaphoreType.DMA((6,)),
        ],
        compiler_params=pltpu.CompilerParams(vmem_limit_bytes=VMEM_LIMIT),
        name="near_output",
    )(mine, theirs, r1, r2, *weights)


def select_gate(modulation, second, text):
    video_cols = modulation[:, 2 * D : 3 * D]
    text_cols = modulation[:, 5 * D : 6 * D]
    video_pick = jnp.where(second, video_cols[1][None, :], video_cols[0][None, :])
    text_pick = jnp.where(second, text_cols[1][None, :], text_cols[0][None, :])
    return jnp.where(text, text_pick, video_pick)


def local(
    tokens, w_query, w_key, w_value, w_out, w_mod, gain_query, gain_key, timesteps,
    video_lengths, piece_table,
):
    x, core = lax.axis_index("x"), lax.axis_index("core")
    z = lax.axis_index("z")
    y = lax.axis_index("yhi") * 2 + lax.axis_index("ylo")
    boundary = TEXT + video_lengths[0]

    across = [tokens] + [shift_x(tokens, step) for step in SHIFTS]
    chunks = across + [swap_core(chunk) for chunk in across]

    w_other = swap_core(w_out)

    act = jax.nn.silu(time_features(timesteps)).astype(BF16)
    part_mod = jnp.dot(act, w_mod, preferred_element_type=F32)
    width = part_mod.shape[1]
    packed = jnp.pad(part_mod.reshape(2 * width), (0, 384 - 2 * width)).reshape(3, 128)
    tiles_axes = ("ylo", "z", "yhi")
    spread = lax.all_to_all(
        jnp.broadcast_to(packed[None], (16, 3, 128)), tiles_axes, 0, 0, tiled=True
    )
    spread = lax.all_to_all(
        jnp.broadcast_to(spread[None], (8, 16, 3, 128)), ("x", "core"), 0, 0, tiled=True
    )
    spread = spread.transpose(1, 0, 2, 3).reshape(128, 384)
    modulation = jnp.stack(
        [spread[:, :width].reshape(128 * width), spread[:, width : 2 * width].reshape(128 * width)]
    )

    back = jnp.array([0, 1, -1, 2], jnp.int32)
    z_ring = (z - back) % 4
    y_ring = (y - back) % 4
    z_tiles = ((y % 2) * 4 + z_ring) * 2 + y // 2
    y_tiles = ((y_ring % 2) * 4 + z) * 2 + y_ring // 2
    tiles = jnp.concatenate([z_tiles, y_tiles])
    pieces = jnp.sum(
        jnp.where(
            tiles[:, None] == jnp.arange(16, dtype=jnp.int32)[None, :], piece_table[None, :], 0
        ),
        axis=1,
    )
    limits_a = jnp.clip(boundary - pieces * CAP, 0, CAP)
    limits_b = jnp.concatenate([limits_a[4:], limits_a[:4]])
    piece = pieces[0]
    x_ring = (x - back) % 4
    starts = jnp.concatenate([(x_ring * 2 + core) * OWN, (x_ring * 2 + 1 - core) * OWN])
    info = jnp.concatenate([starts, jnp.stack([piece, boundary])])

    late_boundary, _ = lax.optimization_barrier((boundary, across[3]))
    cos, sin = rope_tables(piece, late_boundary)
    along_z, along_y = project(
        info, chunks, modulation, w_query, w_key, w_value, cos, sin, gain_query[None, :],
        gain_key[None, :],
    )
    from_z = [along_z] + [shift_z(along_z, step) for step in SHIFTS]
    from_y = [along_y] + [shift_y(along_y, step) for step in SHIFTS]
    limits_a, w_other, w_late, _ = lax.optimization_barrier(
        (limits_a, w_other, w_out, (from_z[1:3], from_y[1:3]))
    )
    w_behind, w_ahead = shift_x(w_late, 1), shift_x(w_late, -1)
    v_behind, v_ahead = swap_core(w_behind), swap_core(w_ahead)
    near_a = attend(limits_a, from_z[:3], from_y[:3], (0, 1, 2), "near_a")[0]
    own_a, *parts_a = attend(limits_a, from_z, from_y, (0, 1, 2, 3), "far_a", near_a)
    sent_a = [shift_z(part, -step) for part, step in zip(parts_a, SHIFTS)]
    limits_b, _ = lax.optimization_barrier((limits_b, parts_a[0]))
    parts_b = attend(limits_b, from_y[1:], from_z, (1, 2, 3), "rest_b")
    sent_b = [shift_y(part, -step) for part, step in zip(parts_b, SHIFTS)]
    limits_b, _ = lax.optimization_barrier((limits_b, (parts_b[0], sent_a)))
    own_b = attend(limits_b, from_y[:1], from_z, (0,), "own_b")[0]

    ahead = (x + back) % 4
    order = jnp.concatenate([(ahead * 2 + 1 - core) * OWN, (ahead * 2 + core) * OWN])
    theirs, mine = merge(order, own_a, sent_a, own_b, sent_b)
    received = swap_core(theirs)
    share = shift_x(far_output(mine, received, w_out, w_other), 2)
    arrived = []
    for i, step in ((1, 1), (2, -1)):
        rows = slice(i * OWN, (i + 1) * OWN)
        arrived.append(shift_x(jnp.concatenate([mine[rows], received[rows]]), step))
    projection = near_output(
        mine, received, *arrived, (w_out, w_other, w_behind, v_behind, w_ahead, v_ahead)
    )
    projection = projection + share.astype(F32)

    own_token = piece * CAP + starts[0] + jnp.arange(OWN, dtype=jnp.int32)[:, None]
    second = own_token >= boundary
    text = own_token - jnp.where(second, boundary, 0) < TEXT
    gate = select_gate(modulation, second, text)
    return (gate * projection).astype(BF16)


def solution(mesh):
    fine = Mesh(mesh.devices.reshape(2, 4, 2, 4, 2), AXES)
    tensor = ("x", "core")
    placed = (
        P(AXES, None),
        P(None, tensor),
        P(None, tensor),
        P(None, tensor),
        P(tensor, None),
        P(None, AXES),
        P(),
        P(),
        P(),
        P(),
        P(),
    )
    return jax.shard_map(
        local, mesh=fine, in_specs=placed, out_specs=P(AXES, None), check_vma=False
    )
```

```python
import functools
import math

import jax
import jax.numpy as jnp
from jax import lax
from jax.experimental import pallas as pl
from jax.experimental.pallas import tpu as pltpu
from jax.sharding import Mesh, PartitionSpec as P

HD = 64
TE = 512
TEXT = 226
HP = 30
WP = 45
CAP = 640
D = 3072
BLK = 128
OWN = 80
BIG = 16384.0
F32 = jnp.float32
BF16 = jnp.bfloat16

AXES = ("ylo", "z", "yhi", "x", "core")
Y_AXES = ("ylo", "yhi")
Y_INDEX = (0, 2, 1, 3)
VMEM_LIMIT = 60 * 1024 * 1024
SHIFTS = (1, -1, 2)


def shift_x(value, step):
    return lax.ppermute(value, "x", [(i, (i + step) % 4) for i in range(4)])


def shift_z(value, step):
    return lax.ppermute(value, "z", [(i, (i + step) % 4) for i in range(4)])


def shift_y(value, step):
    return lax.ppermute(value, Y_AXES, [(Y_INDEX[i], Y_INDEX[(i + step) % 4]) for i in range(4)])


def swap_core(value):
    return lax.ppermute(value, "core", [(0, 1), (1, 0)])


def time_features(timesteps):
    half_dim = TE // 2
    freqs = jnp.exp(-math.log(10000.0) * jnp.arange(half_dim, dtype=F32) / half_dim)
    angles = timesteps.astype(F32)[:, None] * freqs[None, :]
    return jnp.concatenate([jnp.cos(angles), jnp.sin(angles)], axis=1)


def rope_tables(piece, boundary):
    token = piece * CAP + lax.broadcasted_iota(jnp.int32, (CAP, 2 * HD), 0)
    lane = lax.broadcasted_iota(jnp.int32, (CAP, 2 * HD), 1)
    inner = token - jnp.where(token >= boundary, boundary, 0)
    is_text = inner < TEXT
    video = jnp.maximum(inner - TEXT, 0)
    frame = video // (HP * WP)
    height = video // WP % HP
    width = video % WP
    pair = lane % HD // 2
    time_pairs = HD // 8
    space_pairs = 3 * HD // 16
    freq_time = 10000.0 ** (-jnp.arange(0, HD // 4, 2, dtype=F32) / (HD // 4))
    freq_space = 10000.0 ** (-jnp.arange(0, 3 * HD // 8, 2, dtype=F32) / (3 * HD // 8))
    freq = jnp.concatenate([freq_time, freq_space, freq_space])
    freq = jnp.tile(jnp.repeat(freq, 2), 2)[None, :]
    place = jnp.where(
        pair < time_pairs, frame, jnp.where(pair < time_pairs + space_pairs, height, width)
    )
    angle = place.astype(F32) * freq
    cosine = jnp.where(is_text, 1.0, jnp.cos(angle))
    sine = jnp.where(is_text, 0.0, jnp.sin(angle))
    return cosine, jnp.where(lane % 2 == 0, -sine, sine)


def project_kernel(
    info, c0, c1, c2, c3, c4, c5, c6, c7, mods, wq_far, wk_far, wv_far, cos, sin, gq, gk,
    along_z, along_y, rows_in, wq, wk, wv, qa, kva, qb, kvb, middle, sems,
):
    chunks = (c0, c1, c2, c3, c4, c5, c6, c7)
    arrivals = [
        pltpu.make_async_copy(
            chunk, rows_in.at[pl.ds(pl.multiple_of(info[i], 16), OWN), :], sems.at[3 + i]
        )
        for i, chunk in enumerate(chunks)
    ]
    copies = [
        pltpu.make_async_copy(source, target, sems.at[i])
        for i, (source, target) in enumerate(((wq_far, wq), (wk_far, wk), (wv_far, wv)))
    ]
    for copy in arrivals + copies:
        copy.start()
    gain_q = jnp.concatenate([gq[...], gq[...]], axis=1)
    gain_k = jnp.concatenate([gk[...], gk[...]], axis=1)
    for copy in arrivals:
        copy.wait()
    piece = info[8]
    boundary = info[9]
    line = lax.broadcasted_iota(jnp.int32, (256, 128), 0)
    average = jnp.where(
        line % 128 // HD == lax.broadcasted_iota(jnp.int32, (256, 128), 1) // HD, 1.0 / HD, 0.0
    ).astype(BF16)
    even = lax.broadcasted_iota(jnp.int32, (BLK, 128), 1) % 2 == 0

    def head_mean(entries):
        high = entries.astype(BF16)
        low = (entries - high.astype(F32)).astype(BF16)
        return jnp.dot(
            jnp.concatenate([high, low], axis=1), average, preferred_element_type=F32
        )

    def head_prepare(entries, gain, block):
        center = entries - head_mean(entries)
        variance = head_mean(center * center)
        normed = center * lax.rsqrt(variance + 1e-06) * gain
        other = jnp.where(even, pltpu.roll(normed, 127, 1), pltpu.roll(normed, 1, 1))
        place = slice(block * BLK, (block + 1) * BLK)
        return normed * cos[place, :] + other * sin[place, :]

    for block in range(CAP // BLK):
        place = slice(block * BLK, (block + 1) * BLK)
        values = rows_in[place, :].astype(F32)
        center = values - jnp.mean(values, axis=1, keepdims=True)
        variance = jnp.mean(center * center, axis=1, keepdims=True)
        normed = center * lax.rsqrt(variance + 1e-05)
        token = piece * CAP + block * BLK + lax.broadcasted_iota(jnp.int32, (BLK, 1), 0)
        second = token >= boundary
        text = token - jnp.where(second, boundary, 0) < TEXT

        def pick(part):
            video_cols = slice(part * D, (part + 1) * D)
            text_cols = slice((part + 3) * D, (part + 4) * D)
            video_pick = jnp.where(second, mods[1:2, video_cols], mods[0:1, video_cols])
            text_pick = jnp.where(second, mods[1:2, text_cols], mods[0:1, text_cols])
            return jnp.where(text, text_pick, video_pick)

        modded = (normed * (1.0 + pick(1)) + pick(0)).astype(BF16)
        if block == 0:
            for copy in copies:
                copy.wait()
        query = jnp.dot(modded, wq[...], preferred_element_type=F32)
        key = jnp.dot(modded, wk[...], preferred_element_type=F32)
        value = jnp.dot(modded, wv[...], preferred_element_type=F32)
        base = block * 192
        for group in range(3):
            cols = slice(group * 128, (group + 1) * 128)
            q_turn = head_prepare(query[:, cols], gain_q, block).T.astype(BF16)
            v_turn = value[:, cols].T.astype(BF16)
            k_rows = head_prepare(key[:, cols], gain_k, block)
            if group == 0:
                qa[base : base + 128, :] = q_turn
                kva[960 + base : 960 + base + 128, :] = v_turn
                kva[place, :] = k_rows.astype(BF16)
            elif group == 1:
                qa[base + 128 : base + 192, :] = q_turn[:64]
                qb[base + 128 : base + 192, :] = q_turn[64:]
                kva[960 + base + 128 : 960 + base + 192, :] = v_turn[:64]
                kvb[960 + base + 128 : 960 + base + 192, :] = v_turn[64:]
                middle[place, :] = k_rows
            else:
                qb[base : base + 128, :] = q_turn
                kvb[960 + base : 960 + base + 128, :] = v_turn
                kvb[place, :] = k_rows.astype(BF16)
    left = lax.broadcasted_iota(jnp.int32, (CAP // 2, 128), 1) < HD
    upper = middle[: CAP // 2, :]
    lower = middle[CAP // 2 :, :]
    kva[CAP:960, :] = jnp.where(left, upper, pltpu.roll(lower, HD, 1)).astype(BF16)
    kvb[CAP:960, :] = jnp.where(left, pltpu.roll(upper, HD, 1), lower).astype(BF16)
    along_z[:960, :] = qa[...]
    along_z[960:, :] = kvb[...]
    along_y[:960, :] = qb[...]
    along_y[960:, :] = kva[...]


def project(info, chunks, mods, wq, wk, wv, cos, sin, gq, gk):
    vmem = pl.BlockSpec(memory_space=pltpu.VMEM)
    return pl.pallas_call(
        project_kernel,
        out_shape=[jax.ShapeDtypeStruct((2880, 128), BF16)] * 2,
        in_specs=[pl.BlockSpec(memory_space=pltpu.SMEM)]
        + [pl.BlockSpec(memory_space=pl.ANY)] * 8
        + [vmem]
        + [pl.BlockSpec(memory_space=pl.ANY)] * 3
        + [vmem] * 4,
        out_specs=[vmem] * 2,
        scratch_shapes=[pltpu.VMEM((CAP, D), BF16)]
        + [pltpu.VMEM((D, 384), BF16)] * 3
        + [pltpu.VMEM((960, 128), BF16), pltpu.VMEM((1920, 128), BF16)] * 2
        + [pltpu.VMEM((CAP, 128), F32), pltpu.SemaphoreType.DMA((11,))],
        compiler_params=pltpu.CompilerParams(vmem_limit_bytes=VMEM_LIMIT),
        name="project",
    )(info, *chunks, mods, wq, wk, wv, cos, sin, gq, gk)


def attend_kernel(limits, *refs, places, n_k, carried, last):
    n_q = len(places)
    queries, refs = refs[:n_q], refs[n_q:]
    keys, refs = refs[:n_k], refs[n_k:]
    if carried:
        before, refs = refs[0], refs[1:]
    n_out = n_q if last else 1
    outs, refs = refs[:n_out], refs[n_out:]
    qs, ks, vs, todo = refs[:4]
    acc = refs[4] if last else outs[0]
    scale = math.log2(math.e) / math.sqrt(HD)
    half = CAP // 2
    ones = jnp.where(lax.broadcasted_iota(jnp.int32, (16, CAP), 0) == 0, 1.0, 0.0).astype(BF16)
    blank = jnp.zeros((HD, CAP), BF16)

    kinds = [
        jnp.where(limits[4 + tile] == CAP, 0, jnp.where(limits[4 + tile] == 0, 2, 1))
        for tile in range(n_k)
    ]
    slots = []
    only_first = jnp.int32(0)
    only_second = jnp.int32(0)
    key_limit = jnp.int32(0)
    for tile in range(n_k):
        slot = jnp.int32(0)
        for other in range(n_k):
            if other < tile:
                slot = slot + jnp.where(kinds[other] <= kinds[tile], 1, 0)
            elif other > tile:
                slot = slot + jnp.where(kinds[other] < kinds[tile], 1, 0)
        slots.append(slot)
        only_first = only_first + jnp.where(kinds[tile] == 0, 1, 0)
        only_second = only_second + jnp.where(kinds[tile] == 2, 1, 0)
        key_limit = key_limit + limits[4 + tile]
    for i, place in enumerate(places):
        has_first = limits[place] > 0
        has_second = limits[place] < CAP
        todo[16 + i] = limits[place]
        if carried and place != 3:
            shared = (has_first & (limits[7] > 0)) | (has_second & (limits[7] < CAP))
            todo[i] = slots[3]
            todo[8 + i] = jnp.where(shared, 1, 0)
        else:
            low = jnp.where(has_first, 0, only_first)
            todo[i] = low
            todo[8 + i] = jnp.where(has_second, n_k, n_k - only_second) - low

    for tile in range(n_k):
        start = pl.multiple_of(slots[tile] * CAP, 64)
        ks[0, pl.ds(start, CAP), :] = keys[tile][:CAP, :]
        end = keys[tile][CAP:960, :]
        ks[1, pl.ds(start, half), :] = end
        ks[1, pl.ds(start + half, half), :] = jnp.concatenate([end[:, HD:], end[:, :HD]], axis=1)
        vs[pl.ds(pl.multiple_of(slots[tile] * 960, 64), 960), :] = keys[tile][960:, :]
    for i, place in enumerate(places):
        for head in range(3):
            at = HD if head == 1 else 0
            qs[i, head, HD - at : 2 * HD - at, :] = blank
            for block in range(5):
                row = 192 * block + HD * head
                cols = slice(128 * block, 128 * block + 128)
                qs[i, head, at : at + HD, cols] = queries[i][row : row + HD, :]
        if carried and place != 3:
            acc[i] = before[i]
        else:
            acc[i] = jnp.zeros((3, 80, CAP), F32)

    def part(i, head, slot, count, masked):
        first = pl.multiple_of(slot * CAP, 64)
        bank = jnp.where(head == 2, 1, 0)
        scores = jnp.dot(
            ks[bank, pl.ds(first, count * CAP), :], qs[i, head], preferred_element_type=F32
        )
        weights = jnp.exp2(scores * scale).astype(BF16)
        columns = []
        for block in range(5 * count):
            start = slot * 960 + head * HD + 192 * block
            columns.append(vs[pl.ds(pl.multiple_of(start, HD), HD), :])
        value = jnp.concatenate(
            [jnp.concatenate(columns, axis=1), jnp.concatenate([ones] * count, axis=1)], axis=0
        )
        place = first + lax.broadcasted_iota(jnp.int32, value.shape, 1)
        k_second = jnp.where(place >= key_limit, 1, 0)
        nothing = jnp.zeros_like(value)
        if masked:
            value = jnp.concatenate(
                [
                    jnp.where(k_second == 0, value, nothing),
                    jnp.where(k_second == 1, value, nothing),
                ],
                axis=0,
            )
            both = jnp.dot(value, weights, preferred_element_type=F32)
            q_second = lax.broadcasted_iota(jnp.int32, (80, CAP), 1) >= todo[16 + i]
            acc[i, head] += jnp.where(q_second, both[80:], both[:80])
        else:
            sample = jnp.where(todo[16 + i] > 0, 0, 1)
            value = jnp.where(k_second == sample, value, nothing)
            acc[i, head] += jnp.dot(value, weights, preferred_element_type=F32)

    def heads(i, slot, count, masked):
        def one_head(head, rest):
            part(i, head, slot, count, masked)
            return rest

        lax.fori_loop(0, 3, one_head, 0)

    def q_tile(i, carry):
        low = todo[i]
        count = todo[8 + i]
        limit = todo[16 + i]
        mixed = (limit > 0) & (limit < CAP)

        @pl.when(mixed)
        def _():
            size = 2 if last and not carried and n_q == 3 else 1

            def some(step, inner):
                heads(i, low + size * step, size, True)
                return inner

            lax.fori_loop(0, count // size, some, 0)

        @pl.when(jnp.logical_not(mixed))
        def _():
            def two(step, inner):
                heads(i, low + 2 * step, 2, False)
                return inner

            lax.fori_loop(0, count // 2, two, 0)

            @pl.when(count % 2 == 1)
            def _():
                heads(i, low + count - 1, 1, False)

        return carry

    lax.fori_loop(0, n_q, q_tile, 0)
    if last:
        for i, (place, ref) in enumerate(zip(places, outs)):
            if place == 0:
                ref[...] = acc[i]
                continue
            sums = jnp.concatenate([acc[i, head, HD : HD + 1, :] for head in range(3)], axis=0)
            high = sums.astype(BF16)
            low = (sums - high.astype(F32)).astype(BF16)
            for head in range(3):
                ref[HD * head : HD * head + HD, :] = acc[i, head, :HD, :].astype(BF16)
            ref[192:195, :] = high
            ref[195:198, :] = low
            ref[198:208, :] = jnp.zeros((10, CAP), BF16)


def attend(limits, queries, keys, places, name, before=None):
    vmem = pl.BlockSpec(memory_space=pltpu.VMEM)
    n_q, n_k = len(places), len(keys)
    carried = before is not None
    last = n_k == 4
    if last:
        out_shape = [
            jax.ShapeDtypeStruct((208, CAP), BF16)
            if place
            else jax.ShapeDtypeStruct((3, 80, CAP), F32)
            for place in places
        ]
    else:
        out_shape = [jax.ShapeDtypeStruct((n_q, 3, 80, CAP), F32)]
    scratch = [
        pltpu.VMEM((n_q, 3, 128, CAP), BF16),
        pltpu.VMEM((2, n_k * CAP, 128), BF16),
        pltpu.VMEM((n_k * 960, 128), BF16),
        pltpu.SMEM((24,), jnp.int32),
    ]
    if last:
        scratch.append(pltpu.VMEM((n_q, 3, 80, CAP), F32))
    q_spec = pl.BlockSpec((960, 128), lambda i: (0, 0))
    k_spec = pl.BlockSpec((pl.Element(1920), pl.Element(128)), lambda i: (960, 0))
    operands = [limits, *queries, *keys] + ([before] if carried else [])
    specs = [pl.BlockSpec(memory_space=pltpu.SMEM)] + [q_spec] * n_q + [k_spec] * n_k
    return pl.pallas_call(
        functools.partial(attend_kernel, places=places, n_k=n_k, carried=carried, last=last),
        out_shape=out_shape,
        grid=(1,),
        in_specs=specs + [vmem] * (len(operands) - len(specs)),
        out_specs=[vmem] * len(out_shape),
        scratch_shapes=scratch,
        cost_estimate=pl.CostEstimate(flops=1000, transcendentals=0, bytes_accessed=1000),
        compiler_params=pltpu.CompilerParams(vmem_limit_bytes=VMEM_LIMIT),
        name=name,
    )(*operands)


def merge_kernel(
    order, own_a, a1, a2, a3, own_b, b1, b2, b3, theirs, mine, turned, rows
):
    for own, others, heads in (
        (own_a, (a1, a2, a3), (0, 1, 2)),
        (own_b, (b1, b2, b3), (4, 5, 3)),
    ):
        for place, head in enumerate(heads):
            total = own[place, :HD, :]
            share = own[place, HD : HD + 1, :]
            for ref in others:
                total = total + ref[HD * place : HD * place + HD, :].astype(F32)
                tail = ref[192:208, :].astype(F32)
                share = share + tail[place : place + 1, :] + tail[3 + place : 4 + place, :]
            turned[HD * head : HD * head + HD, :] = total / share

    def turn(block, carry):
        place = pl.ds(pl.multiple_of(block * 128, 128), 128)
        for group in range(3):
            cols = slice(group * 128, group * 128 + 128)
            rows[place, cols] = turned[cols, place].T.astype(BF16)
        return carry

    lax.fori_loop(0, 5, turn, 0)
    for i in range(4):
        start = pl.multiple_of(order[i], 16)
        theirs[i * OWN : (i + 1) * OWN, :] = rows[pl.ds(start, OWN), :]
        start = pl.multiple_of(order[4 + i], 16)
        mine[i * OWN : (i + 1) * OWN, :] = rows[pl.ds(start, OWN), :]


def merge(order, own_a, others_a, own_b, others_b):
    vmem = pl.BlockSpec(memory_space=pltpu.VMEM)
    return pl.pallas_call(
        merge_kernel,
        out_shape=[jax.ShapeDtypeStruct((4 * OWN, 384), BF16)] * 2,
        in_specs=[pl.BlockSpec(memory_space=pltpu.SMEM)] + [vmem] * 8,
        out_specs=[vmem] * 2,
        scratch_shapes=[pltpu.VMEM((384, CAP), F32), pltpu.VMEM((CAP, 384), BF16)],
        compiler_params=pltpu.CompilerParams(vmem_limit_bytes=VMEM_LIMIT),
        name="merge",
    )(order, own_a, *others_a, own_b, *others_b)


def far_output_kernel(mine, theirs, w_here, w_other, out):
    rows = slice(3 * OWN, 4 * OWN)

    def step(i, carry):
        cols = pl.ds(pl.multiple_of(i * 768, 128), 768)
        total = jnp.dot(mine[rows, :], w_here[:, cols], preferred_element_type=F32)
        total += jnp.dot(theirs[rows, :], w_other[:, cols], preferred_element_type=F32)
        out[:, cols] = total.astype(BF16)
        return carry

    lax.fori_loop(0, D // 768, step, 0)


def far_output(mine, theirs, w_here, w_other):
    vmem = pl.BlockSpec(memory_space=pltpu.VMEM)
    return pl.pallas_call(
        far_output_kernel,
        out_shape=jax.ShapeDtypeStruct((OWN, D), BF16),
        in_specs=[vmem] * 4,
        out_specs=vmem,
        cost_estimate=pl.CostEstimate(flops=1000, transcendentals=0, bytes_accessed=1000),
        compiler_params=pltpu.CompilerParams(vmem_limit_bytes=VMEM_LIMIT),
        name="far_output",
    )(mine, theirs, w_here, w_other)


def near_output_kernel(mine, theirs, r1, r2, *refs):
    far, out, held, left, sems = refs[:6], refs[6], refs[7], refs[8], refs[9]
    for i, source in enumerate(far):
        pltpu.make_async_copy(source, held.at[i], sems.at[i]).start()
    rows = (mine[:OWN, :], theirs[:OWN, :], r1[:OWN, :], r1[OWN:, :], r2[:OWN, :], r2[OWN:, :])
    for i, entries in enumerate(rows):
        left[i] = entries
    out[...] = jnp.zeros_like(out)

    def step(i, carry):
        pltpu.make_async_copy(far[0], held.at[i], sems.at[i]).wait()
        out[...] += jnp.dot(left[i], held[i], preferred_element_type=F32)
        return carry

    lax.fori_loop(0, 6, step, 0)


def near_output(mine, theirs, r1, r2, weights):
    vmem = pl.BlockSpec(memory_space=pltpu.VMEM)
    return pl.pallas_call(
        near_output_kernel,
        out_shape=jax.ShapeDtypeStruct((OWN, D), F32),
        in_specs=[vmem] * 4 + [pl.BlockSpec(memory_space=pl.ANY)] * 6,
        out_specs=vmem,
        scratch_shapes=[
            pltpu.VMEM((6, 384, D), BF16),
            pltpu.VMEM((6, OWN, 384), BF16),
            pltpu.SemaphoreType.DMA((6,)),
        ],
        compiler_params=pltpu.CompilerParams(vmem_limit_bytes=VMEM_LIMIT),
        name="near_output",
    )(mine, theirs, r1, r2, *weights)


def select_gate(modulation, second, text):
    video_cols = modulation[:, 2 * D : 3 * D]
    text_cols = modulation[:, 5 * D : 6 * D]
    video_pick = jnp.where(second, video_cols[1][None, :], video_cols[0][None, :])
    text_pick = jnp.where(second, text_cols[1][None, :], text_cols[0][None, :])
    return jnp.where(text, text_pick, video_pick)


def local(
    tokens, w_query, w_key, w_value, w_out, w_mod, gain_query, gain_key, timesteps,
    video_lengths, piece_table,
):
    x, core = lax.axis_index("x"), lax.axis_index("core")
    z = lax.axis_index("z")
    y = lax.axis_index("yhi") * 2 + lax.axis_index("ylo")
    boundary = TEXT + video_lengths[0]

    across = [tokens] + [shift_x(tokens, step) for step in SHIFTS]
    chunks = across + [swap_core(chunk) for chunk in across]

    w_other = swap_core(w_out)

    act = jax.nn.silu(time_features(timesteps)).astype(BF16)
    part_mod = jnp.dot(act, w_mod, preferred_element_type=F32)
    width = part_mod.shape[1]
    packed = jnp.pad(part_mod.reshape(2 * width), (0, 384 - 2 * width)).reshape(3, 128)
    tiles_axes = ("ylo", "z", "yhi")
    spread = lax.all_to_all(
        jnp.broadcast_to(packed[None], (16, 3, 128)), tiles_axes, 0, 0, tiled=True
    )
    spread = lax.all_to_all(
        jnp.broadcast_to(spread[None], (8, 16, 3, 128)), ("x", "core"), 0, 0, tiled=True
    )
    spread = spread.transpose(1, 0, 2, 3).reshape(128, 384)
    modulation = jnp.stack(
        [spread[:, :width].reshape(128 * width), spread[:, width : 2 * width].reshape(128 * width)]
    )

    back = jnp.array([0, 1, -1, 2], jnp.int32)
    z_ring = (z - back) % 4
    y_ring = (y - back) % 4
    z_tiles = ((y % 2) * 4 + z_ring) * 2 + y // 2
    y_tiles = ((y_ring % 2) * 4 + z) * 2 + y_ring // 2
    tiles = jnp.concatenate([z_tiles, y_tiles])
    pieces = jnp.sum(
        jnp.where(
            tiles[:, None] == jnp.arange(16, dtype=jnp.int32)[None, :], piece_table[None, :], 0
        ),
        axis=1,
    )
    limits_a = jnp.clip(boundary - pieces * CAP, 0, CAP)
    limits_b = jnp.concatenate([limits_a[4:], limits_a[:4]])
    piece = pieces[0]
    x_ring = (x - back) % 4
    starts = jnp.concatenate([(x_ring * 2 + core) * OWN, (x_ring * 2 + 1 - core) * OWN])
    info = jnp.concatenate([starts, jnp.stack([piece, boundary])])

    cos, sin = rope_tables(piece, boundary)
    along_z, along_y = project(
        info, chunks, modulation, w_query, w_key, w_value, cos, sin, gain_query[None, :],
        gain_key[None, :],
    )
    from_z = [along_z] + [shift_z(along_z, step) for step in SHIFTS]
    from_y = [along_y] + [shift_y(along_y, step) for step in SHIFTS]
    limits_a, w_other, w_late, _ = lax.optimization_barrier(
        (limits_a, w_other, w_out, (from_z[1:3], from_y[1:3]))
    )
    w_behind, w_ahead = shift_x(w_late, 1), shift_x(w_late, -1)
    v_behind, v_ahead = swap_core(w_behind), swap_core(w_ahead)
    near_a = attend(limits_a, from_z[:3], from_y[:3], (0, 1, 2), "near_a")[0]
    own_a, *parts_a = attend(limits_a, from_z, from_y, (0, 1, 2, 3), "far_a", near_a)
    sent_a = [shift_z(part, -step) for part, step in zip(parts_a, SHIFTS)]
    limits_b, _ = lax.optimization_barrier((limits_b, parts_a[0]))
    parts_b = attend(limits_b, from_y[1:], from_z, (1, 2, 3), "rest_b")
    sent_b = [shift_y(part, -step) for part, step in zip(parts_b, SHIFTS)]
    limits_b, _ = lax.optimization_barrier((limits_b, (parts_b[0], sent_a)))
    own_b = attend(limits_b, from_y[:1], from_z, (0,), "own_b")[0]

    ahead = (x + back) % 4
    order = jnp.concatenate([(ahead * 2 + 1 - core) * OWN, (ahead * 2 + core) * OWN])
    theirs, mine = merge(order, own_a, sent_a, own_b, sent_b)
    received = swap_core(theirs)
    share = shift_x(far_output(mine, received, w_out, w_other), 2)
    arrived = []
    for i, step in ((1, 1), (2, -1)):
        rows = slice(i * OWN, (i + 1) * OWN)
        arrived.append(shift_x(jnp.concatenate([mine[rows], received[rows]]), step))
    projection = near_output(
        mine, received, *arrived, (w_out, w_other, w_behind, v_behind, w_ahead, v_ahead)
    )
    projection = projection + share.astype(F32)

    own_token = piece * CAP + starts[0] + jnp.arange(OWN, dtype=jnp.int32)[:, None]
    second = own_token >= boundary
    text = own_token - jnp.where(second, boundary, 0) < TEXT
    gate = select_gate(modulation, second, text)
    return (gate * projection).astype(BF16)


def solution(mesh):
    fine = Mesh(mesh.devices.reshape(2, 4, 2, 4, 2), AXES)
    tensor = ("x", "core")
    placed = (
        P(AXES, None),
        P(None, tensor),
        P(None, tensor),
        P(None, tensor),
        P(tensor, None),
        P(None, AXES),
        P(),
        P(),
        P(),
        P(),
        P(),
    )
    return jax.shard_map(
        local, mesh=fine, in_specs=placed, out_specs=P(AXES, None), check_vma=False
    )
```
